32 devices in a mesh: expert: 16 (over z, y, core), hidden: 2 (over x).
Axes of the slice: x: 2, y: 2, z: 4, core: 2. Of those that a mesh axis runs over, the one named last changes fastest.
Arguments:
- tokens: bfloat16 [2048, 4096], P('expert'), may hold values from -6 to 6
- enc_weight: bfloat16 [4096, 1024], P('expert', 'hidden'), may hold values from -0.09375 to 0.09375
- routes: int32 [2048, 8], P('expert'), may hold values from 0 to 15, all different within a row; in each aligned block of 128 rows (0 to 127, 128 to 255, ...) at most 128 rows name the same one
- gates: float32 [2048, 8], P('expert'), may hold values from 0.1 to 1
- gate_weight: bfloat16 [16, 1024, 1536], P('expert', None, 'hidden'), may hold values from -0.1875 to 0.1875
- up_weight: bfloat16 [16, 1024, 1536], P('expert', None, 'hidden'), may hold values from -0.1875 to 0.1875
- down_weight: bfloat16 [16, 1536, 1024], P('expert', None, 'hidden'), may hold values from -0.15625 to 0.15625
- dec_weight: bfloat16 [1024, 4096], P('expert', 'hidden'), may hold values from -0.1875 to 0.1875
Outputs:
- mixed: bfloat16 [2048, 4096], P('expert', 'hidden')
The draws below stay inside these ranges and needn't reach their ends.
Inputs may be any that keep to these rules, and one draw needn't show every extreme that they name: `routes`: each row names 8 different experts; within one group of 128 consecutive tokens no expert is named more than 128 times.
All inputs are finite; a program needn't handle non-finite values.
Results may differ from the reference program's by a relative error of at most 0.0076.
Values may be sent and summed in bfloat16 or wider, within the bound.
A program may use at most 64 MiB of HBM per device.

```python
import math
import jax
import jax.numpy as jnp
import numpy as np
from jax import lax

D = 4096
LATENT = 1024
FF = 1536
TOP = 8
TOK_DEV = 128
EXPERTS = 16
TOKENS = 2048
CAP = 128
N_EXPERT = 16


def steps_of(rng, shape, split, smallest, largest):
    gain = 1.0
    for axis_at, parts in split:
        heights = jax.random.uniform(jax.random.fold_in(jax.random.fold_in(rng, 6), axis_at), (parts,), jnp.float32, smallest / len(split), largest / len(split))
        gain = gain * jnp.repeat(jnp.exp(heights), shape[axis_at] // parts).reshape((-1,) + (1,) * (len(shape) - 1 - axis_at))
    return gain


def assign_block(stream_key, own, number, rows, number_of, top, reach, slope):
    ranking = jax.random.permutation(stream_key, number_of)
    crowded, ordinary = portions_of(number_of, rows * top, reach, slope, True), portions_of(number_of, rows * top, reach, slope, False)
    places = jnp.arange(number_of)

    def named(lengths, turn):
        used = int((lengths > 0).sum())
        fixed = max(1, used // 4)
        moved = fixed + (places - fixed + turn * (used - fixed)) % max(1, number_of - fixed)
        return jnp.zeros((number_of,), jnp.int32).at[ranking[jnp.where(places < fixed, places, moved)]].set(jnp.asarray(lengths, jnp.int32))

    lengths = jnp.where(number % 4 == 0, named(crowded, number // 4), named(ordinary, number - number // 4 - 1))
    mixed = jax.random.permutation(jax.random.fold_in(own, 3), number_of)
    source_of, sink = mixed[0:number_of // 2 * 2:2], mixed[1:number_of // 2 * 2:2]
    room = jnp.minimum(lengths[source_of] - 1, reach - lengths[sink]) // 2
    room = jnp.where((source_of == ranking[0]) | (sink == ranking[0]) | (lengths[sink] == 0), 0, jnp.maximum(room, 0))
    moved = jax.random.randint(jax.random.fold_in(own, 4), (number_of // 2,), 0, 1 << 20) % (room + 1)
    lengths = lengths.at[source_of].add(-moved).at[sink].add(moved)
    items = jnp.searchsorted(jnp.cumsum(lengths), jnp.arange(rows * top), side="right").astype(jnp.int32)
    listing = items.reshape(top, rows).T
    listing = listing[jax.random.permutation(jax.random.fold_in(own, 1), rows)]
    turn = jax.random.randint(jax.random.fold_in(own, 2), (rows, 1), 0, top)
    return jnp.take_along_axis(listing, (jnp.arange(top)[None, :] + turn) % top, axis=1)


def portions_of(count, total, limit, skew, full):
    portions = [(1 << 20) // math.isqrt(grade ** skew) + 1 for grade in range(1, count + 1)]
    largest = limit if full else min(limit, max(-(-total // count), total * portions[0] // sum(portions)))
    least = 1 if total - largest >= count - 1 else 0
    counts, spare = [largest] + [least] * (count - 1), total - largest - least * (count - 1)
    while spare > 0:
        movable = [i for i in range(1, count) if counts[i] < largest] or [i for i in range(1, count) if counts[i] < limit]
        pool, budget = sum([portions[i] for i in movable]), spare
        for i in movable:
            addition = min(limit - counts[i], max(1, budget * portions[i] // pool), spare)
            counts[i] = counts[i] + addition
            spare = spare - addition
    return np.array(counts)


def normal_values(own_key, dims, deviation, limit, cuts=(), kind=jnp.bfloat16):
    loudness = steps_of(own_key, dims, cuts, -0.22, 0.18) if cuts else 1.0
    drawn = jax.random.normal(own_key, dims, jnp.float32) * deviation * loudness
    return jnp.minimum(jnp.maximum(drawn, -limit), limit).astype(kind)


def setup_inputs(seed: int = 0) -> dict:
    streams_of = jax.random.split(jax.random.key(seed), 9)
    tokens = normal_values(streams_of[0], (TOKENS, D), 1.0, 6.0, ((0, 16),))
    enc_weight = normal_values(streams_of[1], (D, LATENT), D ** -0.5, 0.09375, ((0, 16), (1, 2)))
    routes_keys = jax.random.split(jax.random.fold_in(streams_of[2], 1), TOKENS // TOK_DEV)
    routes_turns = jax.random.permutation(jax.random.fold_in(streams_of[2], 3), TOKENS // TOK_DEV)
    routes = jax.vmap(lambda own, number: assign_block(jax.random.fold_in(streams_of[2], 2), own, number, TOK_DEV, EXPERTS, TOP, CAP, 2))(routes_keys, routes_turns).reshape((TOKENS, TOP))
    gates = jnp.clip(0.1 + 0.9 * jax.random.uniform(streams_of[3], (TOKENS, TOP), jnp.float32) ** steps_of(streams_of[3], (TOKENS, TOP), ((0, 16),), -0.2, 0.2), 0.1, 1.0)
    gate_weight = normal_values(streams_of[4], (EXPERTS, LATENT, FF), LATENT ** -0.5, 0.1875, ((0, 16), (2, 2)))
    up_weight = normal_values(streams_of[5], (EXPERTS, LATENT, FF), LATENT ** -0.5, 0.1875, ((0, 16), (2, 2)))
    down_weight = normal_values(streams_of[6], (EXPERTS, FF, LATENT), FF ** -0.5, 0.15625, ((0, 16), (2, 2)))
    dec_weight = normal_values(streams_of[7], (LATENT, D), LATENT ** -0.5, 0.1875, ((0, 16), (1, 2)))
    return {"tokens": tokens, "enc_weight": enc_weight, "routes": routes, "gates": gates, "gate_weight": gate_weight, "up_weight": up_weight, "down_weight": down_weight, "dec_weight": dec_weight}


def reference(tokens, enc_weight, routes, gates, gate_weight, up_weight, down_weight, dec_weight):
    latent = jnp.dot(tokens, enc_weight, preferred_element_type=jnp.float32).astype(jnp.bfloat16)
    group_count = TOKENS // TOK_DEV
    blocked = routes.reshape(group_count, TOK_DEV * TOP)

    def ranks(chosen):
        onehot = (chosen[:, None] == jnp.arange(EXPERTS, dtype=jnp.int32)[None, :]).astype(jnp.int32)
        earlier = jnp.cumsum(onehot, axis=0) - onehot
        return jnp.sum(earlier * onehot, axis=1).astype(jnp.int32)

    position = lax.map(ranks, blocked)
    group_ids = jnp.arange(group_count, dtype=jnp.int32)[:, None]
    slot_rows = N_EXPERT * CAP
    target = (blocked * slot_rows + group_ids * CAP + position).reshape(-1).astype(jnp.int32)
    source_row = (jnp.arange(TOKENS * TOP, dtype=jnp.int32) // TOP).astype(jnp.int32)
    slots = jnp.zeros((EXPERTS * slot_rows, LATENT), jnp.bfloat16).at[target].set(latent[source_row])
    slots = slots.reshape(EXPERTS, slot_rows, LATENT)

    def expert(inputs):
        arrived, gate_matrix, up_matrix, down_matrix = inputs
        gate_part = jnp.dot(arrived, gate_matrix, preferred_element_type=jnp.float32)
        up_part = jnp.dot(arrived, up_matrix, preferred_element_type=jnp.float32)
        activation = (jax.nn.silu(gate_part) * up_part).astype(jnp.bfloat16)
        return jnp.dot(activation, down_matrix, preferred_element_type=jnp.float32).astype(jnp.bfloat16)

    answer = lax.map(expert, (slots, gate_weight, up_weight, down_weight)).reshape(EXPERTS * slot_rows, LATENT)
    picked = answer[target].astype(jnp.float32).reshape(TOKENS, TOP, LATENT)
    combined = jnp.sum(picked * gates[:, :, None], axis=1).astype(jnp.bfloat16)
    return jnp.dot(combined, dec_weight, preferred_element_type=jnp.float32).astype(jnp.bfloat16)
```

```python
import jax
import jax.numpy as jnp
from jax import lax
from jax.experimental import pallas as pl
from jax.experimental.pallas import tpu as pltpu
from jax.sharding import PartitionSpec as P


def exchange_slots(tokens, enc_weight, routes, gates, gate_weight, up_weight, down_weight, dec_weight):
    groups = lax.axis_size("expert")
    token_count, choice_count = routes.shape
    capacity = min(token_count, 2 * token_count * choice_count // groups)
    columns = tokens
    latent = jnp.dot(
        columns,
        lax.all_gather(enc_weight, "expert", axis=0, tiled=True),
        preferred_element_type=jnp.float32,
    ).astype(jnp.bfloat16)
    payload = lax.all_gather(latent, "hidden", axis=1, tiled=True)
    chosen = routes.reshape(-1)
    onehot = (chosen[:, None] == jnp.arange(groups, dtype=jnp.int32)[None, :]).astype(jnp.int32)
    position = jnp.sum((jnp.cumsum(onehot, axis=0) - onehot) * onehot, axis=1)
    target = chosen * capacity + position
    source_row = jnp.arange(token_count * choice_count, dtype=jnp.int32) // choice_count
    payload_width = payload.shape[1]
    outgoing = (
        jnp.zeros((groups * capacity, payload_width), jnp.bfloat16)
        .at[target]
        .set(payload[source_row])
    )
    outgoing = outgoing.reshape(groups, capacity, payload_width)
    gate_matrix = gate_weight[0]
    up_matrix = up_weight[0]
    down_matrix = down_weight[0]
    arrived = lax.all_to_all(outgoing, "expert", split_axis=0, concat_axis=0, tiled=True)
    slot_count = arrived.shape[1]
    inputs = arrived.reshape(groups * slot_count, arrived.shape[2])
    gate_part = jnp.dot(inputs, gate_matrix, preferred_element_type=jnp.float32)
    up_part = jnp.dot(inputs, up_matrix, preferred_element_type=jnp.float32)
    activation = (jax.nn.silu(gate_part) * up_part).astype(jnp.bfloat16)
    answer = jnp.dot(
        lax.all_gather(activation, "hidden", axis=1, tiled=True),
        down_matrix,
        preferred_element_type=jnp.float32,
    ).astype(jnp.bfloat16)
    answer = answer.reshape(groups, slot_count, down_matrix.shape[1])
    returned_rows = lax.all_to_all(answer, "expert", split_axis=0, concat_axis=0, tiled=True)
    returned_rows = returned_rows.reshape(groups * capacity, returned_rows.shape[2])
    picked = returned_rows[target].astype(jnp.float32).reshape(token_count, choice_count, -1)
    combined = jnp.sum(picked * gates[:, :, None], axis=1).astype(jnp.bfloat16)
    combined_all = lax.all_gather(combined, "hidden", axis=1, tiled=True)
    columns = combined_all
    return jnp.dot(
        columns,
        lax.all_gather(dec_weight, "expert", axis=0, tiled=True),
        preferred_element_type=jnp.float32,
    ).astype(jnp.bfloat16)


CORES, LINES = 2, 2
MESH = pl.DeviceIdType.MESH


CHUNKS, PIECES = 2, 4
LATENT_FIRST = ((1, 0), (1, 0), (1, 0), (1, 0))
ANSWER_FIRST = ((0, 0), (0, 0), (0, 0), (0, 0))


def layer_kernel(
    tokens_hbm, enc_hbm, routes, gates, gate_hbm, up_hbm, down_hbm, dec_hbm, out,
    tok, gate, up, down, enc_all, dec_all, latents, table, shares_in, shares, acc, part_out, part_in, activation,
    answers, core_in, one_out, one_in, two_out, two_in, keep, z_out, z_in, combined, mixed, result,
    ssem, rsem, enc_z, lat_z, share_sem, dec_sem, z_sem, local_sem,
):
    groups = lax.axis_size("expert")
    depth = groups // (CORES * LINES)
    e = lax.axis_index("expert")
    h = lax.axis_index("hidden")
    c, y, z = e % CORES, (e // CORES) % LINES, e // (CORES * LINES)

    def at(zz, yy, cc):
        return (zz * LINES + yy) * CORES + cc

    orders = []
    for zz in range(depth):
        others = [o for o in range(depth) if o != zz]
        middle = (depth - 1) / 2
        orders.append([zz] + sorted(others, key=lambda o: (abs(o - zz), abs(o - middle))))
    nearest = []
    for s in range(depth):
        pick = jnp.int32(orders[0][s])
        for zz in range(1, depth):
            pick = jnp.where(z == zz, orders[zz][s], pick)
        nearest.append(pick)

    rows = tok.shape[1] // 2
    wide = tok.shape[2]
    chunk = latents.shape[3]
    half = chunk * CHUNKS
    band = LINES * CORES * rows
    last = depth - 1
    y_peer = (at(z, 1 - y, c), h)
    core_peer = (at(z, y, 1 - c), h)
    x_peer = (e, 1 - h)

    def route(pair, cc):
        along_y = jnp.where(cc == 0, pair[0], pair[1]) == 1
        first = (jnp.where(along_y, at(z, 1 - y, c), e), jnp.where(along_y, h, 1 - h))
        second = (jnp.where(along_y, e, at(z, 1 - y, c)), jnp.where(along_y, 1 - h, h))
        f = (jnp.where(along_y, 1 - y, y), jnp.where(along_y, h, 1 - h))
        g = (jnp.where(along_y, y, 1 - y), jnp.where(along_y, 1 - h, h))
        return first, second, f, g

    waiting, slots, local = [], {}, []

    def slot(*key):
        return rsem.at[slots.setdefault(key, len(slots))]

    def send(src, dst, sem, peer, when=None):
        copy = pltpu.make_async_remote_copy(
            src_ref=src, dst_ref=dst, send_sem=ssem.at[len(waiting)], recv_sem=sem,
            device_id=peer, device_id_type=MESH,
        )
        if when is None:
            copy.start()
        else:
            pl.when(when)(copy.start)
        waiting.append((copy, when))

    def along(zz):
        return (at(jnp.clip(zz, 0, depth - 1), y, c), h)

    ending = jnp.logical_or(z == 0, z == depth - 1)

    def spread(block, sem, far=(1, 2), when=True):
        for d in far:
            send(block, block, sem, along(z + d), jnp.logical_and(when, z + d < depth))
            send(block, block, sem, along(z - d), jnp.logical_and(when, z - d >= 0))

    def hand_on(block, sem, zz):
        send(block, block, sem, along(z + 1), jnp.logical_and(z - zz == 2, z + 1 < depth))
        send(block, block, sem, along(z - 1), jnp.logical_and(zz - z == 2, z - 1 >= 0))

    def arrive(dst, sem):
        pltpu.make_async_copy(dst, dst, sem).wait()

    def fetch(src, dst):
        copy = pltpu.make_async_copy(src, dst, local_sem.at[len(local)])
        copy.start()
        local.append(copy)
        return copy

    barrier = pltpu.get_barrier_semaphore()
    peers = [((e + d) % groups, h) for d in range(1, groups)] + [x_peer]
    for peer in peers:
        pl.semaphore_signal(barrier, inc=1, device_id=peer, device_id_type=MESH)

    def segment(zz, yy):
        return pl.ds(pl.multiple_of((zz * LINES + yy) * wide, wide), wide)

    enc_own = [
        fetch(enc_hbm.at[:, pl.ds(k * chunk, chunk)], enc_all.at[k, z, c]) for k in range(CHUNKS)
    ]
    tok_own = [fetch(tokens_hbm.at[:, segment(zz, y)], tok.at[zz, pl.ds(0, rows)]) for zz in range(depth)]
    dec_own = fetch(dec_hbm, dec_all.at[e])
    part = down.shape[1]
    gate_own = fetch(gate_hbm.at[0], gate)
    up_own = fetch(up_hbm.at[0], up)
    own_down = fetch(down_hbm.at[0, pl.ds(pl.multiple_of(h * part, part), part)], down.at[h])

    expert = lax.broadcasted_iota(jnp.int32, (groups, rows), 0)
    weight = jnp.zeros((groups, rows), jnp.float32)
    for k in range(routes.shape[0]):
        weight += jnp.where(routes[k : k + 1, :] == expert, gates[k : k + 1, :], 0.0)
    for o in range(groups):
        table[o] = jnp.broadcast_to(weight[o : o + 1, :], table.shape[1:])

    pl.semaphore_wait(barrier, len(peers))

    def enc_block(k, zz, cc):
        return enc_all.at[k, zz, cc]

    def enc_start(k):
        block = enc_block(k, z, c)
        enc_own[k].wait()
        if k == 0:
            spread(block, enc_z.at[k, z])
        else:
            spread(block, enc_z.at[k, z], (1,))
            spread(block, enc_z.at[k, z], (2,), ending)
        send(block, block, slot("enc", k, 0), core_peer)

    def enc_later(k):
        spread(enc_block(k, z, c), enc_z.at[k, z], (2,), jnp.logical_not(ending))

    def enc_from_z(k, s):
        zz = nearest[s]
        block = enc_block(k, zz, c)
        arrive(block, enc_z.at[k, zz])
        if s == last:
            hand_on(block, enc_z.at[k, zz], zz)
        send(block, block, slot("enc", k, s), core_peer)

    def tok_block(zz):
        return tok.at[zz, pl.ds(rows, rows)]

    def tok_send(s):
        zz = nearest[s]
        send(tokens_hbm.at[:, segment(zz, 1 - y)], tok_block(zz), slot("tok", s), y_peer)

    def tok_wait(s):
        arrive(tok_block(nearest[s]), slot("tok", s))

    def enc_step(k, s):
        zz = nearest[s]
        arrive(enc_block(k, zz, 1 - c), slot("enc", k, s))
        p = jnp.dot(tok[zz], enc_all[k, zz].reshape(wide, chunk), preferred_element_type=jnp.float32)
        if s == 0:
            acc[k] = p
        else:
            acc[k] = acc[k] + p

    def enc_share(k):
        part_out[k] = acc[k, rows:, :].astype(jnp.bfloat16)
        send(part_out.at[k], part_in.at[k], slot("part", k), y_peer)

    def lat_block(k, zz, yy, cc, hh):
        return latents.at[hh, k, pl.ds(pl.multiple_of(at(zz, yy, cc) * rows, rows), rows)]

    def enc_done(k):
        arrive(part_in.at[k], slot("part", k))
        own = acc[k, :rows, :] + part_in[k].astype(jnp.float32)
        latents[h, k, pl.ds(pl.multiple_of(e * rows, rows), rows), :] = own.astype(jnp.bfloat16)

    def lat_from_z(k, s):
        zz = nearest[s]
        block = lat_block(k, zz, y, c, h)
        if s == 0:
            spread(block, lat_z.at[k, zz])
        else:
            arrive(block, lat_z.at[k, zz])
            if s == last:
                hand_on(block, lat_z.at[k, zz], zz)
        first, second, _, _ = route(LATENT_FIRST[s % 4], c)
        send(block, block, slot("lat1", k, s), first)
        send(block, block, slot("lat2", k, s), second)
        send(block, block, slot("lat3", k, s, 0), core_peer)

    def lat_from_first(k, s):
        _, second, f, _ = route(LATENT_FIRST[s % 4], c)
        block = lat_block(k, nearest[s], f[0], c, f[1])
        arrive(block, slot("lat1", k, s))
        send(block, block, slot("lat4", k, s), second)
        send(block, block, slot("lat3", k, s, 1), core_peer)

    def lat_from_second(k, s):
        _, _, _, g = route(LATENT_FIRST[s % 4], c)
        block = lat_block(k, nearest[s], g[0], c, g[1])
        arrive(block, slot("lat2", k, s))
        send(block, block, slot("lat3", k, s, 2), core_peer)
        block = lat_block(k, nearest[s], 1 - y, c, 1 - h)
        arrive(block, slot("lat4", k, s))
        send(block, block, slot("lat3", k, s, 3), core_peer)

    def lat_from_core(k, s):
        _, _, f, g = route(LATENT_FIRST[s % 4], 1 - c)
        for i, (yy, hh) in enumerate(((y, h), f, g, (1 - y, 1 - h))):
            arrive(lat_block(k, nearest[s], yy, 1 - c, hh), slot("lat3", k, s, i))

    def dec_block(o):
        return dec_all.at[o]

    def dec_send(o, peer):
        send(dec_block(o), dec_block(o), dec_sem.at[o], peer)

    def dec_start_z():
        spread(dec_block(e), dec_sem.at[e])

    def dec_start_y():
        dec_own.wait()
        dec_send(e, y_peer)
        dec_send(e, core_peer)

    def dec_from_z(s):
        zz = nearest[s]
        o = at(zz, y, c)
        arrive(dec_block(o), dec_sem.at[o])
        if s == last:
            hand_on(dec_block(o), dec_sem.at[o], zz)
        dec_send(o, y_peer)
        dec_send(o, core_peer)

    def dec_from_y(s):
        o = at(nearest[s], 1 - y, c)
        arrive(dec_block(o), dec_sem.at[o])
        dec_send(o, core_peer)

    def dec_from_core(s):
        for yy in (y, 1 - y):
            o = at(nearest[s], yy, 1 - c)
            arrive(dec_block(o), dec_sem.at[o])

    piece = part // PIECES

    def down_rows(hh, i, base):
        return pl.ds(pl.multiple_of(base * part + i * piece, piece), piece)

    def down_send(i):
        send(
            down_hbm.at[0, down_rows(h, i, 1 - h)], down.at[h, pl.ds(i * piece, piece)],
            slot("down", i), x_peer,
        )

    def down_wait():
        own_down.wait()
        for i in range(PIECES):
            arrive(down.at[1 - h, pl.ds(i * piece, piece)], slot("down", i))

    def share_start():
        for d in range(1, groups):
            o = (e + d) % groups
            send(table.at[o], shares_in.at[e], share_sem.at[e], (o, h))
        shares_in[e] = table[e]

    def share_done():
        for d in range(1, groups):
            o = (e + d) % groups
            arrive(shares_in.at[o], share_sem.at[o])
        tiles = [shares_in[nearest[s] * LINES * CORES + b] for s in range(depth) for b in range(LINES * CORES)]
        shares[...] = jnp.concatenate(tiles, axis=0).T

    tile = 256

    def gate_up(s, where):
        start = pl.multiple_of(nearest[s] * band, band)

        @pl.loop(0, gate.shape[1] // tile)
        def _(n):
            columns = pl.ds(pl.multiple_of(n * tile, tile), tile)
            parts = [latents[hh, k, pl.ds(start, band), :] for hh in range(2) for k in range(CHUNKS)]
            inputs = jnp.concatenate(parts, axis=1)
            g = jnp.dot(inputs, gate[:, columns], preferred_element_type=jnp.float32)
            u = jnp.dot(inputs, up[:, columns], preferred_element_type=jnp.float32)
            activation[where, :, columns] = (g / (1.0 + jnp.exp(-g)) * u).astype(jnp.bfloat16)

    def answer_rows(s, where):
        for hh in (1 - h, h):
            @pl.loop(0, half // tile)
            def _(n):
                columns = pl.ds(pl.multiple_of(n * tile, tile), tile)
                a = jnp.dot(activation[where], down[hh, :, columns], preferred_element_type=jnp.float32)
                for b in range(LINES * CORES):
                    j = (s * LINES * CORES + b) * 8
                    share = shares[:, j : j + 1]
                    answers[s, b, hh, :, columns] = (a[b * rows : (b + 1) * rows] * share).astype(jnp.bfloat16)

            for yy in range(LINES):
                send(
                    answers.at[s, yy * CORES + 1 - c, hh], core_in.at[s, yy, hh],
                    slot("core", s, yy, 0 if hh is not h else 1), core_peer,
                )

    def both(s, yy, hh):
        return answers[s, yy * CORES + c, hh].astype(jnp.float32) + core_in[s, yy, hh].astype(jnp.float32)

    def sum_cores(s):
        first, _, f, _ = route(ANSWER_FIRST[s % 4], c)
        for i, hh in enumerate((1 - h, h)):
            for yy in range(LINES):
                arrive(core_in.at[s, yy, hh], slot("core", s, yy, i))
        for i, (yy, hh) in enumerate(((1 - y, 1 - h), f)):
            one_out[s, i] = both(s, yy, hh).astype(jnp.bfloat16)
            send(one_out.at[s, i], one_in.at[s, i], slot("one", s, i), first)

    def sum_first(s):
        _, second, _, g = route(ANSWER_FIRST[s % 4], c)
        arrive(one_in.at[s, 0], slot("one", s, 0))
        two_out[s] = (both(s, g[0], g[1]) + one_in[s, 0].astype(jnp.float32)).astype(jnp.bfloat16)
        send(two_out.at[s], two_in.at[s], slot("two", s), second)
        arrive(one_in.at[s, 1], slot("one", s, 1))
        keep[s] = both(s, y, h) + one_in[s, 1].astype(jnp.float32)

    def sum_second(s):
        arrive(two_in.at[s], slot("two", s))
        total = keep[s] + two_in[s].astype(jnp.float32)
        if s == 0:
            keep[s] = total
        else:
            z_out[s] = total.astype(jnp.bfloat16)
            peer = (at(nearest[s], y, c), h)
            send(z_out.at[s], z_in.at[z], z_sem.at[z], peer)

    enc_start(0)
    for s in range(depth):
        tok_send(s)
    for i in range(PIECES):
        down_send(i)
    share_start()
    enc_from_z(0, 1)
    enc_start(1)
    for copy in tok_own:
        copy.wait()
    enc_from_z(0, 2)
    tok_wait(0)
    enc_step(0, 0)
    tok_wait(1)
    enc_step(0, 1)
    enc_from_z(0, 3)
    enc_later(1)
    tok_wait(2)
    enc_step(0, 2)
    tok_wait(3)
    enc_step(0, 3)
    enc_share(0)
    dec_start_y()
    enc_from_z(1, 1)
    enc_step(1, 0)
    enc_from_z(1, 2)
    enc_step(1, 1)
    enc_step(1, 2)
    enc_done(0)
    lat_from_z(0, 0)
    enc_from_z(1, 3)
    enc_step(1, 3)
    enc_share(1)
    lat_from_z(0, 1)
    lat_from_first(0, 0)
    lat_from_z(0, 2)
    lat_from_first(0, 1)
    lat_from_second(0, 0)
    lat_from_z(0, 3)
    enc_done(1)
    lat_from_z(1, 0)
    lat_from_first(0, 2)
    lat_from_second(0, 1)
    lat_from_z(1, 1)
    lat_from_first(0, 3)
    lat_from_second(0, 2)
    lat_from_first(1, 0)
    lat_from_z(1, 2)
    lat_from_second(0, 3)
    lat_from_first(1, 1)
    lat_from_second(1, 0)
    share_done()
    gate_own.wait()
    up_own.wait()
    lat_from_z(1, 3)
    dec_start_z()
    lat_from_core(0, 0)
    lat_from_core(1, 0)
    gate_up(0, 0)
    lat_from_first(1, 2)
    lat_from_second(1, 1)
    lat_from_core(0, 1)
    lat_from_core(1, 1)
    gate_up(1, 1)
    lat_from_first(1, 3)
    lat_from_second(1, 2)
    down_wait()
    answer_rows(1, 1)
    lat_from_core(0, 2)
    lat_from_core(1, 2)
    sum_cores(1)
    gate_up(2, 1)
    lat_from_second(1, 3)
    dec_from_z(1)
    answer_rows(2, 1)
    lat_from_core(0, 3)
    lat_from_core(1, 3)
    sum_first(1)
    sum_cores(2)
    gate_up(3, 1)
    dec_from_z(2)
    sum_second(1)
    answer_rows(3, 1)
    sum_first(2)
    sum_cores(3)
    answer_rows(0, 0)
    dec_from_z(3)
    sum_second(2)
    sum_first(3)
    sum_cores(0)
    for s in range(depth):
        dec_from_y(s)
    sum_second(3)
    sum_first(0)
    final = jnp.zeros((rows, half), jnp.float32)
    for s in range(1, depth):
        arrive(z_in.at[nearest[s]], z_sem.at[nearest[s]])
        final += z_in[nearest[s]].astype(jnp.float32)
    keep[1] = final
    for s in range(depth):
        dec_from_core(s)
    sum_second(0)
    combined[h] = (keep[0] + keep[1]).astype(jnp.bfloat16)
    send(combined.at[h], combined.at[h], slot("last"), x_peer)

    per = groups // 2

    def product(hh, columns):
        block = dec_all[pl.ds(pl.multiple_of(hh * per, per), per), :, columns].reshape(half, tile)
        return jnp.dot(combined[hh], block, preferred_element_type=jnp.float32)

    @pl.loop(0, mixed.shape[1] // tile)
    def _(n):
        columns = pl.ds(pl.multiple_of(n * tile, tile), tile)
        mixed[:, columns] = product(h, columns)

    arrive(combined.at[1 - h], slot("last"))
    stored = []
    for i in range(2):
        width = mixed.shape[1] // 2

        @pl.loop(0, width // tile)
        def _(n):
            columns = pl.ds(pl.multiple_of(i * width + n * tile, tile), tile)
            result[:, columns] = (mixed[:, columns] + product(1 - h, columns)).astype(jnp.bfloat16)

        stored.append(fetch(result.at[:, pl.ds(i * width, width)], out.at[:, pl.ds(i * width, width)]))

    for copy, when in waiting:
        if when is None:
            copy.wait_send()
        else:
            pl.when(when)(copy.wait_send)
    for copy in stored:
        copy.wait()


def whole_layer(tokens, enc_weight, routes, gates, gate_weight, up_weight, down_weight, dec_weight):
    groups = lax.axis_size("expert")
    depth = groups // (CORES * LINES)
    rows, width = tokens.shape
    half = enc_weight.shape[1]
    hidden = gate_weight.shape[2]
    bf, f32 = jnp.bfloat16, jnp.float32
    band = LINES * CORES
    chunk = half // CHUNKS
    anywhere = pl.BlockSpec(memory_space=pl.ANY)
    vmem = pl.BlockSpec(memory_space=pltpu.VMEM)
    dma = pltpu.SemaphoreType.DMA
    scratch = [
        pltpu.VMEM((depth, 2 * rows, width // (LINES * depth)), bf),
        pltpu.VMEM(gate_weight.shape[1:], bf),
        pltpu.VMEM(up_weight.shape[1:], bf),
        pltpu.VMEM((2, hidden, half), bf),
        pltpu.VMEM((CHUNKS, depth, CORES, enc_weight.shape[0], chunk), bf),
        pltpu.VMEM((groups, *dec_weight.shape), bf),
        pltpu.VMEM((2, CHUNKS, groups * rows, chunk), bf),
        pltpu.VMEM((groups, 8, rows), f32),
        pltpu.VMEM((groups, 8, rows), f32),
        pltpu.VMEM((rows, groups * 8), f32),
        pltpu.VMEM((CHUNKS, 2 * rows, chunk), f32),
        pltpu.VMEM((CHUNKS, rows, chunk), bf),
        pltpu.VMEM((CHUNKS, rows, chunk), bf),
        pltpu.VMEM((2, band * rows, hidden), bf),
        pltpu.VMEM((depth, band, 2, rows, half), bf),
        pltpu.VMEM((depth, LINES, 2, rows, half), bf),
        pltpu.VMEM((depth, 2, rows, half), bf),
        pltpu.VMEM((depth, 2, rows, half), bf),
        pltpu.VMEM((depth, rows, half), bf),
        pltpu.VMEM((depth, rows, half), bf),
        pltpu.VMEM((depth, rows, half), f32),
        pltpu.VMEM((depth, rows, half), bf),
        pltpu.VMEM((depth, rows, half), bf),
        pltpu.VMEM((2, rows, half), bf),
        pltpu.VMEM((rows, dec_weight.shape[1]), f32),
        pltpu.VMEM((rows, dec_weight.shape[1]), bf),
        dma((256,)), dma((160,)), dma((CHUNKS, depth)), dma((CHUNKS, depth)),
        dma((groups,)), dma((groups,)), dma((depth,)), dma((16,)),
    ]
    return pl.pallas_call(
        layer_kernel,
        out_shape=jax.ShapeDtypeStruct((rows, dec_weight.shape[1]), bf),
        in_specs=[anywhere, anywhere, vmem, vmem, anywhere, anywhere, anywhere, anywhere],
        out_specs=anywhere,
        scratch_shapes=scratch,
        compiler_params=pltpu.CompilerParams(
            collective_id=0, has_side_effects=True, vmem_limit_bytes=60 * 1024 * 1024
        ),
    )(tokens, enc_weight, routes.T, gates.T, gate_weight, up_weight, down_weight, dec_weight)


def on_device(tokens, enc_weight, routes, *rest):
    token_count, choice_count = routes.shape
    plan = whole_layer if 2 * choice_count >= lax.axis_size("expert") else exchange_slots
    return plan(tokens, enc_weight, routes, *rest)


def solution(mesh):
    in_specs = (
        P("expert", None),
        P("expert", "hidden"),
        P("expert", None),
        P("expert", None),
        P("expert", None, "hidden"),
        P("expert", None, "hidden"),
        P("expert", None, "hidden"),
        P("expert", "hidden"),
    )
    out_specs = P("expert", "hidden")
    return jax.shard_map(
        on_device, mesh=mesh, in_specs=in_specs, out_specs=out_specs, check_vma=False
    )
```

```python
import jax
import jax.numpy as jnp
from jax import lax
from jax.experimental import pallas as pl
from jax.experimental.pallas import tpu as pltpu
from jax.sharding import PartitionSpec as P


def exchange_slots(tokens, enc_weight, routes, gates, gate_weight, up_weight, down_weight, dec_weight):
    groups = lax.axis_size("expert")
    token_count, choice_count = routes.shape
    capacity = min(token_count, 2 * token_count * choice_count // groups)
    columns = tokens
    latent = jnp.dot(
        columns,
        lax.all_gather(enc_weight, "expert", axis=0, tiled=True),
        preferred_element_type=jnp.float32,
    ).astype(jnp.bfloat16)
    payload = lax.all_gather(latent, "hidden", axis=1, tiled=True)
    chosen = routes.reshape(-1)
    onehot = (chosen[:, None] == jnp.arange(groups, dtype=jnp.int32)[None, :]).astype(jnp.int32)
    position = jnp.sum((jnp.cumsum(onehot, axis=0) - onehot) * onehot, axis=1)
    target = chosen * capacity + position
    source_row = jnp.arange(token_count * choice_count, dtype=jnp.int32) // choice_count
    payload_width = payload.shape[1]
    outgoing = (
        jnp.zeros((groups * capacity, payload_width), jnp.bfloat16)
        .at[target]
        .set(payload[source_row])
    )
    outgoing = outgoing.reshape(groups, capacity, payload_width)
    gate_matrix = gate_weight[0]
    up_matrix = up_weight[0]
    down_matrix = down_weight[0]
    arrived = lax.all_to_all(outgoing, "expert", split_axis=0, concat_axis=0, tiled=True)
    slot_count = arrived.shape[1]
    inputs = arrived.reshape(groups * slot_count, arrived.shape[2])
    gate_part = jnp.dot(inputs, gate_matrix, preferred_element_type=jnp.float32)
    up_part = jnp.dot(inputs, up_matrix, preferred_element_type=jnp.float32)
    activation = (jax.nn.silu(gate_part) * up_part).astype(jnp.bfloat16)
    answer = jnp.dot(
        lax.all_gather(activation, "hidden", axis=1, tiled=True),
        down_matrix,
        preferred_element_type=jnp.float32,
    ).astype(jnp.bfloat16)
    answer = answer.reshape(groups, slot_count, down_matrix.shape[1])
    returned_rows = lax.all_to_all(answer, "expert", split_axis=0, concat_axis=0, tiled=True)
    returned_rows = returned_rows.reshape(groups * capacity, returned_rows.shape[2])
    picked = returned_rows[target].astype(jnp.float32).reshape(token_count, choice_count, -1)
    combined = jnp.sum(picked * gates[:, :, None], axis=1).astype(jnp.bfloat16)
    combined_all = lax.all_gather(combined, "hidden", axis=1, tiled=True)
    columns = combined_all
    return jnp.dot(
        columns,
        lax.all_gather(dec_weight, "expert", axis=0, tiled=True),
        preferred_element_type=jnp.float32,
    ).astype(jnp.bfloat16)


CORES, LINES = 2, 2
MESH = pl.DeviceIdType.MESH


CHUNKS, HALVES, PAIR, PIECES, STEPS = 2, 2, 2, 4, 2
LATENT_FIRST = ((1, 0), (1, 0), (1, 0), (1, 0))
ANSWER_FIRST = ((0, 1), (0, 1), (0, 1), (0, 1))


def layer_kernel(
    tokens_hbm, enc_hbm, routes, gates, gate_hbm, up_hbm, down_hbm, dec_hbm, out,
    tok, gate, up, down, enc_all, dec_all, latents, table, shares_in, shares, acc, part_out, part_in, activation,
    answers, core_in, one_out, one_in, two_out, two_in, keep, own, z_out, z_in, combined, mixed, part_mixed, mixed_in, result,
    ssem, rsem, lat_z, share_sem, dec_sem, z_sem, local_sem,
):
    groups = lax.axis_size("expert")
    depth = groups // (CORES * LINES)
    e = lax.axis_index("expert")
    h = lax.axis_index("hidden")
    c, y, z = e % CORES, (e // CORES) % LINES, e // (CORES * LINES)

    def at(zz, yy, cc):
        return (zz * LINES + yy) * CORES + cc

    orders = []
    for zz in range(depth):
        others = [o for o in range(depth) if o != zz]
        middle = (depth - 1) / 2
        orders.append([zz] + sorted(others, key=lambda o: (abs(o - zz), abs(o - middle))))
    nearest = []
    for s in range(depth):
        pick = jnp.int32(orders[0][s])
        for zz in range(1, depth):
            pick = jnp.where(z == zz, orders[zz][s], pick)
        nearest.append(pick)

    rows = tok.shape[2] // 2
    wide = tok.shape[3]
    few = latents.shape[2] // groups
    half = latents.shape[3]
    chunk = half // CHUNKS
    band = LINES * CORES * few
    last = depth - 1
    y_peer = (at(z, 1 - y, c), h)
    core_peer = (at(z, y, 1 - c), h)
    x_peer = (e, 1 - h)

    def route(pair, cc):
        along_y = jnp.where(cc == 0, pair[0], pair[1]) == 1
        first = (jnp.where(along_y, at(z, 1 - y, c), e), jnp.where(along_y, h, 1 - h))
        second = (jnp.where(along_y, e, at(z, 1 - y, c)), jnp.where(along_y, 1 - h, h))
        f = (jnp.where(along_y, 1 - y, y), jnp.where(along_y, h, 1 - h))
        g = (jnp.where(along_y, y, 1 - y), jnp.where(along_y, 1 - h, h))
        return first, second, f, g

    waiting, slots, local = [], {}, []

    def slot(*key):
        return rsem.at[slots.setdefault(key, len(slots))]

    def send(src, dst, sem, peer, when=None):
        copy = pltpu.make_async_remote_copy(
            src_ref=src, dst_ref=dst, send_sem=ssem.at[len(waiting)], recv_sem=sem,
            device_id=peer, device_id_type=MESH,
        )
        if when is None:
            copy.start()
        else:
            pl.when(when)(copy.start)
        waiting.append((copy, when))

    def along(zz):
        return (at(jnp.clip(zz, 0, depth - 1), y, c), h)

    def spread(block, sem, far):
        for d in far:
            send(block, block, sem, along(z + d), z + d < depth)
            send(block, block, sem, along(z - d), z - d >= 0)

    def arrive(dst, sem):
        pltpu.make_async_copy(dst, dst, sem).wait()

    def fetch(src, dst):
        copy = pltpu.make_async_copy(src, dst, local_sem.at[len(local)])
        copy.start()
        local.append(copy)
        return copy

    barrier = pltpu.get_barrier_semaphore()
    peers = [((e + d) % groups, h) for d in range(1, groups)] + [x_peer]
    for peer in peers:
        pl.semaphore_signal(barrier, inc=1, device_id=peer, device_id_type=MESH)

    def segment(zz, yy):
        return pl.ds(pl.multiple_of((zz * LINES + yy) * wide, wide), wide)

    enc_own = [
        fetch(enc_hbm.at[:, pl.ds(k * chunk, chunk)], enc_all.at[k, 0, y, c]) for k in range(CHUNKS)
    ]
    pair, twin = z + 1 - 2 * (z % 2), (z + depth // 2) % depth
    planes, pair_planes = (z, twin), (pair, (pair + depth // 2) % depth)
    tok_own = [
        fetch(tokens_hbm.at[:, segment(planes[j], yy)], tok.at[j, yy, pl.ds(0, rows)])
        for j in range(2) for yy in range(LINES)
    ]
    dec_own = fetch(dec_hbm, dec_all.at[z, c])
    part = down.shape[1]
    gate_own = fetch(gate_hbm.at[0], gate)
    up_own = fetch(up_hbm.at[0], up)
    own_down = fetch(down_hbm.at[0, pl.ds(pl.multiple_of(h * part, part), part)], down.at[h])

    expert = lax.broadcasted_iota(jnp.int32, (groups, rows), 0)
    weight = jnp.zeros((groups, rows), jnp.float32)
    for k in range(routes.shape[0]):
        weight += jnp.where(routes[k : k + 1, :] == expert, gates[k : k + 1, :], 0.0)
    for o in range(groups):
        table[o] = jnp.broadcast_to(weight[o : o + 1, :], table.shape[1:])

    pl.semaphore_wait(barrier, len(peers))

    def enc_block(k, j, yy, cc):
        return enc_all.at[k, j, yy, cc]

    def enc_start(k):
        block = enc_block(k, 0, y, c)
        enc_own[k].wait()
        send(block, enc_block(k, 1, y, c), slot("encz", k), along(twin))
        send(block, block, slot("ency", k, 0), y_peer)
        send(block, block, slot("encc", k, 0, 0), core_peer)

    def enc_from_z(k):
        block = enc_block(k, 1, y, c)
        arrive(block, slot("encz", k))
        send(block, block, slot("ency", k, 1), y_peer)
        send(block, block, slot("encc", k, 1, 0), core_peer)

    def enc_from_y(k, j):
        block = enc_block(k, j, 1 - y, c)
        arrive(block, slot("ency", k, j))
        send(block, block, slot("encc", k, j, 1), core_peer)

    def tok_block(j, yy):
        return tok.at[j, yy, pl.ds(rows, rows)]

    def tok_send(j, i):
        yy = y if i == 0 else 1 - y
        send(tokens_hbm.at[:, segment(pair_planes[j], yy)], tok_block(j, yy), slot("tok", j, i), along(pair))

    def tok_wait(j):
        for i, yy in enumerate((y, 1 - y)):
            arrive(tok_block(j, yy), slot("tok", j, i))

    def enc_step(k, j):
        for i, yy in enumerate((y, 1 - y)):
            arrive(enc_block(k, j, yy, 1 - c), slot("encc", k, j, i))
        columns = slice(k * chunk, (k + 1) * chunk)
        for i in range(LINES):
            p = jnp.dot(tok[j, i], enc_all[k, j, i].reshape(wide, chunk), preferred_element_type=jnp.float32)
            if i + j == 0:
                acc[:, columns] = p
            else:
                acc[:, columns] = acc[:, columns] + p

    def enc_share(k):
        part_out[k] = acc[rows + k * few : rows + (k + 1) * few, :].astype(jnp.bfloat16)
        send(part_out.at[k], part_in.at[k], slot("part", k), along(pair))

    def lat_block(k, zz, yy, cc, hh):
        return latents.at[hh, k, pl.ds(pl.multiple_of(at(zz, yy, cc) * few, few), few)]

    def enc_done(k):
        arrive(part_in.at[k], slot("part", k))
        mine = acc[k * few : (k + 1) * few, :] + part_in[k].astype(jnp.float32)
        latents[h, k, pl.ds(pl.multiple_of(e * few, few), few), :] = mine.astype(jnp.bfloat16)
        block = lat_block(k, z, y, c, h)
        spread(block, lat_z.at[k, z], range(1, depth))

    def lat_from_z(k, s):
        zz = nearest[s]
        block = lat_block(k, zz, y, c, h)
        if s > 0:
            arrive(block, lat_z.at[k, zz])
        first, second, _, _ = route(LATENT_FIRST[s % 4], c)
        send(block, block, slot("lat1", k, s), first)
        send(block, block, slot("lat2", k, s), second)
        send(block, block, slot("lat3", k, s, 0), core_peer)

    def lat_from_first(k, s):
        _, second, f, _ = route(LATENT_FIRST[s % 4], c)
        block = lat_block(k, nearest[s], f[0], c, f[1])
        arrive(block, slot("lat1", k, s))
        send(block, block, slot("lat4", k, s), second)
        send(block, block, slot("lat3", k, s, 1), core_peer)

    def lat_from_second(k, s):
        _, _, _, g = route(LATENT_FIRST[s % 4], c)
        block = lat_block(k, nearest[s], g[0], c, g[1])
        arrive(block, slot("lat2", k, s))
        send(block, block, slot("lat3", k, s, 2), core_peer)
        block = lat_block(k, nearest[s], 1 - y, c, 1 - h)
        arrive(block, slot("lat4", k, s))
        send(block, block, slot("lat3", k, s, 3), core_peer)

    def lat_from_core(k, s):
        _, _, f, g = route(LATENT_FIRST[s % 4], 1 - c)
        for i, (yy, hh) in enumerate(((y, h), f, g, (1 - y, 1 - h))):
            arrive(lat_block(k, nearest[s], yy, 1 - c, hh), slot("lat3", k, s, i))

    def dec_block(zz, cc):
        return dec_all.at[zz, cc]

    def dec_middle():
        block, beyond = dec_block(z, c), z - 1 + 2 * (z % 2)
        dec_own.wait()
        send(block, block, dec_sem.at[z], along(beyond), jnp.logical_and(beyond >= 0, beyond < depth))

    def dec_near():
        block = dec_block(z, c)
        send(block, block, dec_sem.at[z], along(pair))
        send(block, block, slot("dec", 0), core_peer)

    def dec_far():
        spread(dec_block(z, c), dec_sem.at[z], range(2, depth))

    def dec_from_z(s):
        zz = nearest[s]
        arrive(dec_block(zz, c), dec_sem.at[zz])
        send(dec_block(zz, c), dec_block(zz, c), slot("dec", s), core_peer)

    def dec_from_core(s):
        arrive(dec_block(nearest[s], 1 - c), slot("dec", s))

    piece = part // PIECES

    def down_rows(hh, i, base):
        return pl.ds(pl.multiple_of(base * part + i * piece, piece), piece)

    def down_send(i):
        send(
            down_hbm.at[0, down_rows(h, i, 1 - h)], down.at[h, pl.ds(i * piece, piece)],
            slot("down", i), x_peer,
        )

    def down_wait():
        own_down.wait()
        for i in range(PIECES):
            arrive(down.at[1 - h, pl.ds(i * piece, piece)], slot("down", i))

    def share_start():
        for d in range(1, groups):
            o = (e + d) % groups
            send(table.at[o], shares_in.at[e], share_sem.at[e], (o, h))
        shares_in[e] = table[e]

    def share_done():
        for d in range(1, groups):
            o = (e + d) % groups
            arrive(shares_in.at[o], share_sem.at[o])
        tiles = [shares_in[nearest[s] * LINES * CORES + b] for s in range(depth) for b in range(LINES * CORES)]
        shares[...] = jnp.concatenate(tiles, axis=0).T

    group = CORES * dec_all.shape[2]
    tile = LINES * group

    stages = [(k, u) for k in range(HALVES) for u in range(depth // PAIR)[:: 1 - 2 * k]]

    def gate_up(s, where):
        k, u = stages[s]
        starts = [pl.multiple_of(nearest[u * PAIR + i] * band, band) for i in range(PAIR)]

        @pl.loop(0, gate.shape[1] // tile)
        def _(n):
            columns = pl.ds(pl.multiple_of(n * tile, tile), tile)
            parts = [
                jnp.concatenate([latents[hh, k, pl.ds(start, band), :] for hh in range(2)], axis=1) for start in starts
            ]
            inputs = jnp.concatenate(parts, axis=0)
            g = jnp.dot(inputs, gate[:, columns], preferred_element_type=jnp.float32)
            u = jnp.dot(inputs, up[:, columns], preferred_element_type=jnp.float32)
            activation[where, :, columns] = (g / (1.0 + jnp.exp(-g)) * u).astype(jnp.bfloat16)

    def answer_rows(s, where):
        k, u = stages[s]
        for i, hh in enumerate((1 - h, h)):
            @pl.loop(0, half // tile)
            def _(n):
                columns = pl.ds(pl.multiple_of(n * tile, tile), tile)
                a = jnp.dot(activation[where], down[hh, :, columns], preferred_element_type=jnp.float32)
                for m in range(PAIR):
                    for b in range(LINES * CORES):
                        start = (m * LINES * CORES + b) * few
                        j = ((u * PAIR + m) * LINES * CORES + b) * 8
                        block = a[start : start + few] * shares[k * few : (k + 1) * few, j : j + 1]
                        for yy in range(LINES):
                            answers[
                                s, b % CORES, yy, hh, pl.ds((m * LINES + b // CORES) * few, few),
                                pl.ds(pl.multiple_of(n * group, group), group),
                            ] = block[:, yy * group : (yy + 1) * group].astype(jnp.bfloat16)

            for yy in range(LINES):
                send(
                    answers.at[s, 1 - c, yy, hh], core_in.at[s, yy, hh], slot("core", s, yy, i), core_peer,
                )

    def both(s, yy, hh):
        return answers[s, c, yy, hh].astype(jnp.float32) + core_in[s, yy, hh].astype(jnp.float32)

    def sum_cores(s):
        first, _, f, _ = route(ANSWER_FIRST[s % 4], c)
        for i, hh in enumerate((1 - h, h)):
            for yy in range(LINES):
                arrive(core_in.at[s, yy, hh], slot("core", s, yy, i))
        for i, (yy, hh) in enumerate(((1 - y, 1 - h), f)):
            one_out[s, i] = both(s, yy, hh).astype(jnp.bfloat16)
            send(one_out.at[s, i], one_in.at[s, i], slot("one", s, i), first)

    def sum_first(s):
        _, second, _, g = route(ANSWER_FIRST[s % 4], c)
        arrive(one_in.at[s, 0], slot("one", s, 0))
        two_out[s] = (both(s, g[0], g[1]) + one_in[s, 0].astype(jnp.float32)).astype(jnp.bfloat16)
        send(two_out.at[s], two_in.at[s], slot("two", s), second)
        arrive(one_in.at[s, 1], slot("one", s, 1))
        keep[s] = both(s, y, h) + one_in[s, 1].astype(jnp.float32)

    def sum_second(s):
        k, u = stages[s]
        arrive(two_in.at[s], slot("two", s))
        total = keep[s] + two_in[s].astype(jnp.float32)
        rest = total.shape[0] // PAIR
        if u == 0:
            own[k] = total[:rest]
        for i in range(PAIR):
            if u + i > 0:
                z_out[s, i] = total[i * rest : (i + 1) * rest].astype(jnp.bfloat16)
                send(z_out.at[s, i], z_in.at[z, k], z_sem.at[z, k], along(nearest[u * PAIR + i]))

    per = depth // 2
    width = part_mixed.shape[3]

    def product(k, hh, columns):
        block = dec_all[pl.ds(pl.multiple_of(hh * per, per), per), :, :, columns].reshape(half // LINES, width)
        return jnp.dot(combined[k, hh], block, preferred_element_type=jnp.float32)

    def combine(k):
        final = own[k]
        for s in range(1, depth):
            arrive(z_in.at[nearest[s], k], z_sem.at[nearest[s], k])
            final += z_in[nearest[s], k].astype(jnp.float32)
        combined[k, h] = final.astype(jnp.bfloat16)
        send(combined.at[k, h], combined.at[k, h], slot("last", k), x_peer)

    def mix(k):
        for n in range(STEPS):
            columns = slice(n * width, (n + 1) * width)
            mixed[k, :, columns] = product(k, h, columns)
        arrive(combined.at[k, 1 - h], slot("last", k))
        theirs = pl.ds(pl.multiple_of((1 - y) * few, few), few)
        for n in range(STEPS):
            columns = slice(n * width, (n + 1) * width)
            mixed[k, :, columns] = mixed[k, :, columns] + product(k, 1 - h, columns)
            part_mixed[k, n] = mixed[k, theirs, columns].astype(jnp.bfloat16)
            send(part_mixed.at[k, n], mixed_in.at[k, n], slot("mixed", k, n), y_peer)

    stored = []

    def store(k):
        mine = pl.ds(pl.multiple_of(y * few, few), few)
        for n in range(STEPS):
            columns = slice(n * width, (n + 1) * width)
            arrive(mixed_in.at[k, n], slot("mixed", k, n))
            result[k, :, columns] = (mixed[k, mine, columns] + mixed_in[k, n].astype(jnp.float32)).astype(jnp.bfloat16)
            window = (pl.ds(k * few, few), pl.ds(n * width, width))
            stored.append(fetch(result.at[k, :, pl.ds(n * width, width)], out.at[window]))

    tok_send(0, 0)
    enc_start(0)
    tok_send(0, 1)
    for i in range(PIECES):
        down_send(i)
    share_start()
    enc_start(1)
    tok_send(1, 0)
    tok_send(1, 1)
    for copy in tok_own:
        copy.wait()
    enc_from_y(0, 0)
    enc_from_z(0)
    enc_from_y(1, 0)
    enc_from_y(0, 1)
    tok_wait(0)
    enc_step(0, 0)
    enc_step(1, 0)
    enc_from_z(1)
    dec_middle()
    enc_from_y(1, 1)
    tok_wait(1)
    enc_step(0, 1)
    enc_step(1, 1)
    enc_share(0)
    enc_share(1)
    enc_done(0)
    lat_from_z(0, 0)
    enc_done(1)
    lat_from_z(1, 0)
    dec_near()
    dec_far()
    lat_from_first(0, 0)
    lat_from_z(0, 1)
    lat_from_first(1, 0)
    lat_from_z(0, 2)
    lat_from_first(0, 1)
    lat_from_z(0, 3)
    share_done()
    gate_own.wait()
    up_own.wait()
    lat_from_second(0, 0)
    lat_from_first(0, 2)
    lat_from_second(0, 1)
    lat_from_z(1, 1)
    lat_from_core(0, 0)
    lat_from_core(0, 1)
    gate_up(0, 0)
    lat_from_z(1, 2)
    lat_from_first(0, 3)
    lat_from_first(1, 1)
    lat_from_z(1, 3)
    lat_from_second(0, 2)
    down_wait()
    answer_rows(0, 0)
    lat_from_first(1, 2)
    lat_from_second(0, 3)
    lat_from_second(1, 0)
    lat_from_second(1, 1)
    lat_from_first(1, 3)
    sum_cores(0)
    lat_from_core(0, 2)
    lat_from_core(0, 3)
    gate_up(1, 1)
    lat_from_second(1, 2)
    lat_from_second(1, 3)
    answer_rows(1, 1)
    sum_first(0)
    lat_from_core(1, 2)
    lat_from_core(1, 3)
    sum_cores(1)
    gate_up(2, 0)
    sum_second(0)
    answer_rows(2, 0)
    lat_from_core(1, 0)
    lat_from_core(1, 1)
    sum_first(1)
    sum_cores(2)
    gate_up(3, 1)
    sum_second(1)
    answer_rows(3, 1)
    sum_first(2)
    sum_cores(3)
    for s in range(1, depth):
        dec_from_z(s)
    sum_second(2)
    sum_first(3)
    combine(0)
    for s in range(depth):
        dec_from_core(s)
    sum_second(3)
    mix(0)
    combine(1)
    mix(1)
    store(0)
    store(1)

    for copy, when in waiting:
        if when is None:
            copy.wait_send()
        else:
            pl.when(when)(copy.wait_send)
    for copy in stored:
        copy.wait()


def whole_layer(tokens, enc_weight, routes, gates, gate_weight, up_weight, down_weight, dec_weight):
    groups = lax.axis_size("expert")
    depth = groups // (CORES * LINES)
    rows, width = tokens.shape
    half = enc_weight.shape[1]
    hidden = gate_weight.shape[2]
    bf, f32 = jnp.bfloat16, jnp.float32
    band = LINES * CORES
    chunk = half // CHUNKS
    few = rows // HALVES
    columns = dec_weight.shape[1]
    block = (PAIR * LINES * few, half // LINES)
    small = (LINES * few, half // LINES)
    anywhere = pl.BlockSpec(memory_space=pl.ANY)
    vmem = pl.BlockSpec(memory_space=pltpu.VMEM)
    dma = pltpu.SemaphoreType.DMA
    scratch = [
        pltpu.VMEM((2, LINES, 2 * rows, width // (LINES * depth)), bf),
        pltpu.VMEM(gate_weight.shape[1:], bf),
        pltpu.VMEM(up_weight.shape[1:], bf),
        pltpu.VMEM((2, hidden, half), bf),
        pltpu.VMEM((CHUNKS, 2, LINES, CORES, enc_weight.shape[0], chunk), bf),
        pltpu.VMEM((depth, CORES, *dec_weight.shape), bf),
        pltpu.VMEM((2, HALVES, groups * few, half), bf),
        pltpu.VMEM((groups, 8, rows), f32),
        pltpu.VMEM((groups, 8, rows), f32),
        pltpu.VMEM((rows, groups * 8), f32),
        pltpu.VMEM((2 * rows, half), f32),
        pltpu.VMEM((HALVES, few, half), bf),
        pltpu.VMEM((HALVES, few, half), bf),
        pltpu.VMEM((2, PAIR * band * few, hidden), bf),
        pltpu.VMEM((depth, CORES, LINES, 2, *block), bf),
        pltpu.VMEM((depth, LINES, 2, *block), bf),
        pltpu.VMEM((depth, 2, *block), bf),
        pltpu.VMEM((depth, 2, *block), bf),
        pltpu.VMEM((depth, *block), bf),
        pltpu.VMEM((depth, *block), bf),
        pltpu.VMEM((depth, *block), f32),
        pltpu.VMEM((HALVES, *small), f32),
        pltpu.VMEM((depth, PAIR, *small), bf),
        pltpu.VMEM((depth, HALVES, *small), bf),
        pltpu.VMEM((HALVES, 2, *small), bf),
        pltpu.VMEM((HALVES, LINES * few, columns), f32),
        pltpu.VMEM((HALVES, STEPS, few, columns // STEPS), bf),
        pltpu.VMEM((HALVES, STEPS, few, columns // STEPS), bf),
        pltpu.VMEM((HALVES, few, columns), bf),
        dma((256,)), dma((160,)), dma((HALVES, depth)),
        dma((groups,)), dma((depth,)), dma((depth, HALVES)), dma((16,)),
    ]
    return pl.pallas_call(
        layer_kernel,
        out_shape=jax.ShapeDtypeStruct((rows, dec_weight.shape[1]), bf),
        in_specs=[anywhere, anywhere, vmem, vmem, anywhere, anywhere, anywhere, anywhere],
        out_specs=anywhere,
        scratch_shapes=scratch,
        compiler_params=pltpu.CompilerParams(
            collective_id=0, has_side_effects=True, vmem_limit_bytes=60 * 1024 * 1024
        ),
    )(tokens, enc_weight, routes.T, gates.T, gate_weight, up_weight, down_weight, dec_weight)


def on_device(tokens, enc_weight, routes, *rest):
    token_count, choice_count = routes.shape
    plan = whole_layer if 2 * choice_count >= lax.axis_size("expert") else exchange_slots
    return plan(tokens, enc_weight, routes, *rest)


def solution(mesh):
    in_specs = (
        P("expert", None),
        P("expert", "hidden"),
        P("expert", None),
        P("expert", None),
        P("expert", None, "hidden"),
        P("expert", None, "hidden"),
        P("expert", None, "hidden"),
        P("expert", "hidden"),
    )
    out_specs = P("expert", "hidden")
    return jax.shard_map(
        on_device, mesh=mesh, in_specs=in_specs, out_specs=out_specs, check_vma=False
    )
```

```python
import jax
import jax.numpy as jnp
from jax import lax
from jax.experimental import pallas as pl
from jax.experimental.pallas import tpu as pltpu
from jax.sharding import PartitionSpec as P


def exchange_slots(tokens, enc_weight, routes, gates, gate_weight, up_weight, down_weight, dec_weight):
    groups = lax.axis_size("expert")
    token_count, choice_count = routes.shape
    capacity = min(token_count, 2 * token_count * choice_count // groups)
    columns = tokens
    latent = jnp.dot(
        columns,
        lax.all_gather(enc_weight, "expert", axis=0, tiled=True),
        preferred_element_type=jnp.float32,
    ).astype(jnp.bfloat16)
    payload = lax.all_gather(latent, "hidden", axis=1, tiled=True)
    chosen = routes.reshape(-1)
    onehot = (chosen[:, None] == jnp.arange(groups, dtype=jnp.int32)[None, :]).astype(jnp.int32)
    position = jnp.sum((jnp.cumsum(onehot, axis=0) - onehot) * onehot, axis=1)
    target = chosen * capacity + position
    source_row = jnp.arange(token_count * choice_count, dtype=jnp.int32) // choice_count
    payload_width = payload.shape[1]
    outgoing = (
        jnp.zeros((groups * capacity, payload_width), jnp.bfloat16)
        .at[target]
        .set(payload[source_row])
    )
    outgoing = outgoing.reshape(groups, capacity, payload_width)
    gate_matrix = gate_weight[0]
    up_matrix = up_weight[0]
    down_matrix = down_weight[0]
    arrived = lax.all_to_all(outgoing, "expert", split_axis=0, concat_axis=0, tiled=True)
    slot_count = arrived.shape[1]
    inputs = arrived.reshape(groups * slot_count, arrived.shape[2])
    gate_part = jnp.dot(inputs, gate_matrix, preferred_element_type=jnp.float32)
    up_part = jnp.dot(inputs, up_matrix, preferred_element_type=jnp.float32)
    activation = (jax.nn.silu(gate_part) * up_part).astype(jnp.bfloat16)
    answer = jnp.dot(
        lax.all_gather(activation, "hidden", axis=1, tiled=True),
        down_matrix,
        preferred_element_type=jnp.float32,
    ).astype(jnp.bfloat16)
    answer = answer.reshape(groups, slot_count, down_matrix.shape[1])
    returned_rows = lax.all_to_all(answer, "expert", split_axis=0, concat_axis=0, tiled=True)
    returned_rows = returned_rows.reshape(groups * capacity, returned_rows.shape[2])
    picked = returned_rows[target].astype(jnp.float32).reshape(token_count, choice_count, -1)
    combined = jnp.sum(picked * gates[:, :, None], axis=1).astype(jnp.bfloat16)
    combined_all = lax.all_gather(combined, "hidden", axis=1, tiled=True)
    columns = combined_all
    return jnp.dot(
        columns,
        lax.all_gather(dec_weight, "expert", axis=0, tiled=True),
        preferred_element_type=jnp.float32,
    ).astype(jnp.bfloat16)


CORES, LINES = 2, 2
MESH = pl.DeviceIdType.MESH


CHUNKS, HALVES, PARTS, PIECES, STEPS, RING = 2, 2, 2, 1, 2, 48
LATENT_FIRST = ((1, 0), (1, 0), (1, 0), (1, 0))
ANSWER_FIRST = ((0, 1), (0, 1), (0, 1), (0, 1))


def layer_kernel(
    tokens_hbm, enc_hbm, routes, gates, gate_hbm, up_hbm, down_hbm, dec_hbm, out,
    tok, gate, up, down, enc_all, dec_all, latents, table, shares_in, shares, acc, part_out, part_in, activation,
    answers, core_in, one_out, one_in, two_out, two_in, keep, z_out, z_in, combined, mixed, part_mixed, mixed_in, result,
    ssem, rsem, lat_z, local_sem,
):
    groups = lax.axis_size("expert")
    depth = groups // (CORES * LINES)
    e = lax.axis_index("expert")
    h = lax.axis_index("hidden")
    c, y, z = e % CORES, (e // CORES) % LINES, e // (CORES * LINES)

    def at(zz, yy, cc):
        return (zz * LINES + yy) * CORES + cc

    orders = []
    for zz in range(depth):
        others = [o for o in range(depth) if o != zz]
        middle = (depth - 1) / 2
        orders.append([zz] + sorted(others, key=lambda o: (abs(o - zz), abs(o - middle))))
    nearest = []
    for s in range(depth):
        pick = jnp.int32(orders[0][s])
        for zz in range(1, depth):
            pick = jnp.where(z == zz, orders[zz][s], pick)
        nearest.append(pick)

    rows = tok.shape[2] // 2
    wide = tok.shape[3]
    few, half = latents.shape[3:]
    bit = few // PARTS
    chunk = half // CHUNKS
    last = depth - 1
    y_peer = (at(z, 1 - y, c), h)
    core_peer = (at(z, y, 1 - c), h)
    x_peer = (e, 1 - h)

    def route(pair, cc):
        along_y = jnp.where(cc == 0, pair[0], pair[1]) == 1
        first = (jnp.where(along_y, at(z, 1 - y, c), e), jnp.where(along_y, h, 1 - h))
        second = (jnp.where(along_y, e, at(z, 1 - y, c)), jnp.where(along_y, 1 - h, h))
        f = (jnp.where(along_y, 1 - y, y), jnp.where(along_y, h, 1 - h))
        g = (jnp.where(along_y, y, 1 - y), jnp.where(along_y, 1 - h, h))
        return first, second, f, g

    waiting, lasting, slots, local = [], [], {}, []

    def slot(*key):
        return rsem.at[slots.setdefault(key, len(slots))]

    def sent(copy, when):
        if when is None:
            copy.wait_send()
        else:
            pl.when(when)(copy.wait_send)

    def send(src, dst, sem, peer, when=None, long=False):
        turn = len(waiting)
        if not long and turn >= RING:
            sent(*waiting[turn - RING])
        copy = pltpu.make_async_remote_copy(
            src_ref=src, dst_ref=dst, send_sem=ssem.at[RING + len(lasting) if long else turn % RING], recv_sem=sem,
            device_id=peer, device_id_type=MESH,
        )
        if when is None:
            copy.start()
        else:
            pl.when(when)(copy.start)
        (lasting if long else waiting).append((copy, when))

    def along(zz):
        return (at(jnp.clip(zz, 0, depth - 1), y, c), h)

    def spread(block, sem, far, long=False):
        for d in far:
            send(block, block, sem, along(z + d), z + d < depth, long)
            send(block, block, sem, along(z - d), z - d >= 0, long)

    def arrive(dst, sem):
        pltpu.make_async_copy(dst, dst, sem).wait()

    def fetch(src, dst):
        copy = pltpu.make_async_copy(src, dst, local_sem.at[len(local)])
        copy.start()
        local.append(copy)
        return copy

    barrier = pltpu.get_barrier_semaphore()
    peers = [((e + d) % groups, h) for d in range(1, groups)] + [x_peer]
    for peer in peers:
        pl.semaphore_signal(barrier, inc=1, device_id=peer, device_id_type=MESH)

    def segment(zz, yy):
        return pl.ds(pl.multiple_of((zz * LINES + yy) * wide, wide), wide)

    enc_own = [
        fetch(enc_hbm.at[:, pl.ds(k * chunk, chunk)], enc_all.at[k, 0, y, c]) for k in range(CHUNKS)
    ]
    pair, twin = z + 1 - 2 * (z % 2), (z + depth // 2) % depth
    planes, pair_planes = (z, twin), (pair, (pair + depth // 2) % depth)
    tok_own = [
        fetch(tokens_hbm.at[:, segment(planes[j], yy)], tok.at[j, yy, pl.ds(0, rows)])
        for j in range(2) for yy in range(LINES)
    ]
    dec_own = fetch(dec_hbm, dec_all.at[z, c])
    part = down.shape[1]
    gate_own = fetch(gate_hbm.at[0], gate)
    up_own = fetch(up_hbm.at[0], up)
    own_down = fetch(down_hbm.at[0, pl.ds(pl.multiple_of(h * part, part), part)], down.at[h])

    expert = lax.broadcasted_iota(jnp.int32, (groups, rows), 0)
    weight = jnp.zeros((groups, rows), jnp.float32)
    for k in range(routes.shape[0]):
        weight += jnp.where(routes[k : k + 1, :] == expert, gates[k : k + 1, :], 0.0)
    for o in range(groups):
        table[o] = jnp.broadcast_to(weight[o : o + 1, :], table.shape[1:])

    pl.semaphore_wait(barrier, len(peers))

    def enc_block(k, j, yy, cc):
        return enc_all.at[k, j, yy, cc]

    def enc_start(k):
        block = enc_block(k, 0, y, c)
        enc_own[k].wait()
        send(block, enc_block(k, 1, y, c), slot("encz", k), along(twin))
        send(block, block, slot("ency", k, 0), y_peer)
        send(block, block, slot("encc", k, 0), core_peer)

    def enc_from_z(k):
        block = enc_block(k, 1, y, c)
        arrive(block, slot("encz", k))
        send(block, block, slot("ency", k, 1), y_peer)
        send(block, block, slot("encc", k, 1), core_peer)

    def enc_from_y(k, j):
        block = enc_block(k, j, 1 - y, c)
        arrive(block, slot("ency", k, j))
        send(block, block, slot("encc", k, j), core_peer)

    def tok_block(j, yy):
        return tok.at[j, yy, pl.ds(rows, rows)]

    def tok_send(j, i):
        yy = y if i == 0 else 1 - y
        send(tokens_hbm.at[:, segment(pair_planes[j], yy)], tok_block(j, yy), slot("tok", j), along(pair))

    def tok_wait(j):
        arrive(tok.at[j, :, pl.ds(rows, rows)], slot("tok", j))

    def enc_step(k, j):
        arrive(enc_all.at[k, j, :, 1 - c], slot("encc", k, j))
        columns = slice(k * chunk, (k + 1) * chunk)
        for i in range(LINES):
            p = jnp.dot(tok[j, i], enc_all[k, j, i].reshape(wide, chunk), preferred_element_type=jnp.float32)
            if i + j == 0:
                acc[:, columns] = p
            else:
                acc[:, columns] = acc[:, columns] + p

    def enc_share(k):
        part_out[k] = acc[rows + k * few : rows + (k + 1) * few, :].astype(jnp.bfloat16)
        send(part_out.at[k], part_in.at[k], slot("part", k), along(pair))

    def lat_block(k, zz, yy, cc, hh):
        return latents.at[hh, k, (zz * CORES + cc) * LINES + yy]

    def enc_done(k):
        arrive(part_in.at[k], slot("part", k))
        mine = acc[k * few : (k + 1) * few, :] + part_in[k].astype(jnp.float32)
        latents[h, k, (z * CORES + c) * LINES + y] = mine.astype(jnp.bfloat16)
        block = lat_block(k, z, y, c, h)
        spread(block, lat_z.at[k, z], range(1, depth))

    def lat_from_z(k, s):
        zz = nearest[s]
        block = lat_block(k, zz, y, c, h)
        if s > 0:
            arrive(block, lat_z.at[k, zz])
        first, second, _, _ = route(LATENT_FIRST[s % 4], c)
        send(block, block, slot("lat1", k, s), first)
        send(block, block, slot("lat2", k, s), second)
        send(block, block, slot("lat3", k, s), core_peer)

    def lat_from_first(k, s):
        _, second, f, _ = route(LATENT_FIRST[s % 4], c)
        block = lat_block(k, nearest[s], f[0], c, f[1])
        arrive(block, slot("lat1", k, s))
        send(block, block, slot("lat4", k, s), second)
        send(block, block, slot("lat3", k, s), core_peer)

    def lat_from_second(k, s):
        _, _, _, g = route(LATENT_FIRST[s % 4], c)
        block = lat_block(k, nearest[s], g[0], c, g[1])
        arrive(block, slot("lat2", k, s))
        send(block, block, slot("lat3", k, s), core_peer)
        block = lat_block(k, nearest[s], 1 - y, c, 1 - h)
        arrive(block, slot("lat4", k, s))
        send(block, block, slot("lat3", k, s), core_peer)

    def lat_from_core(k, s):
        start = (nearest[s] * CORES + 1 - c) * LINES
        arrive(latents.at[:, k, pl.ds(start, LINES)], slot("lat3", k, s))

    def dec_block(zz, cc):
        return dec_all.at[zz, cc]

    def dec_middle():
        block, beyond = dec_block(z, c), z - 1 + 2 * (z % 2)
        dec_own.wait()
        send(block, block, slot("decz"), along(beyond), jnp.logical_and(beyond >= 0, beyond < depth), True)

    def dec_near():
        block = dec_block(z, c)
        send(block, block, slot("decz"), along(pair), None, True)
        send(block, block, slot("dec"), core_peer)

    def dec_far():
        spread(dec_block(z, c), slot("decz"), range(2, depth), True)

    def dec_from_z():
        arrive(dec_all.at[pl.ds(0, last), c], slot("decz"))
        for s in range(1, depth):
            block = dec_block(nearest[s], c)
            send(block, block, slot("dec"), core_peer)

    def dec_from_core():
        arrive(dec_all.at[:, 1 - c], slot("dec"))

    piece = part // PIECES

    def down_rows(hh, i, base):
        return pl.ds(pl.multiple_of(base * part + i * piece, piece), piece)

    def down_send(i):
        send(
            down_hbm.at[0, down_rows(h, i, 1 - h)], down.at[h, pl.ds(i * piece, piece)],
            slot("down", i), x_peer, None, True,
        )

    def down_wait():
        own_down.wait()
        for i in range(PIECES):
            arrive(down.at[1 - h, pl.ds(i * piece, piece)], slot("down", i))

    def share_start():
        for d in range(1, groups):
            o = (e + d) % groups
            send(table.at[o], shares_in.at[e], slot("share"), (o, h))
        shares_in[e] = table[e]

    def share_done():
        arrive(shares_in.at[pl.ds(0, groups - 1)], slot("share"))
        shares[...] = jnp.concatenate([shares_in[o] for o in range(groups)], axis=0).T

    group = CORES * dec_all.shape[2]
    tile = LINES * group

    stages = [(k, p) for k in range(HALVES) for p in range(PARTS)]

    def gate_up(s):
        k, p = stages[s]

        @pl.loop(0, gate.shape[1] // tile)
        def _(n):
            columns = pl.ds(pl.multiple_of(n * tile, tile), tile)
            parts = [
                latents[hh, k, :, p * bit : (p + 1) * bit, :].reshape(groups * bit, half) for hh in range(2)
            ]
            inputs = jnp.concatenate(parts, axis=1)
            g = jnp.dot(inputs, gate[:, columns], preferred_element_type=jnp.float32)
            u = jnp.dot(inputs, up[:, columns], preferred_element_type=jnp.float32)
            activation[s % 2, :, columns] = (g / (1.0 + jnp.exp(-g)) * u).astype(jnp.bfloat16)

    def answer_rows(s):
        k, p = stages[s]
        for hh in (1 - h, h):
            @pl.loop(0, half // tile)
            def _(n):
                columns = pl.ds(pl.multiple_of(n * tile, tile), tile)
                a = jnp.dot(activation[s % 2], down[hh, :, columns], preferred_element_type=jnp.float32)
                for b in range(groups):
                    zz, cc, ty = b // (CORES * LINES), b // LINES % CORES, b % LINES
                    j = at(zz, ty, cc) * 8
                    share = shares[k * few + p * bit : k * few + (p + 1) * bit, j : j + 1]
                    block = a[b * bit : (b + 1) * bit] * share
                    for yy in range(LINES):
                        answers[
                            s, cc, yy, hh, pl.ds((zz * LINES + ty) * bit, bit),
                            pl.ds(pl.multiple_of(n * group, group), group),
                        ] = block[:, yy * group : (yy + 1) * group].astype(jnp.bfloat16)

            for yy in range(LINES):
                send(answers.at[s, 1 - c, yy, hh], core_in.at[s, yy, hh], slot("core", s), core_peer)

    def both(s, yy, hh):
        return answers[s, c, yy, hh].astype(jnp.float32) + core_in[s, yy, hh].astype(jnp.float32)

    def sum_cores(s):
        first, _, f, _ = route(ANSWER_FIRST[s % 4], c)
        arrive(core_in.at[s], slot("core", s))
        for i, (yy, hh) in enumerate(((1 - y, 1 - h), f)):
            one_out[s, i] = both(s, yy, hh).astype(jnp.bfloat16)
            send(one_out.at[s, i], one_in.at[s, i], slot("one", s), first)

    def sum_first(s):
        _, second, _, g = route(ANSWER_FIRST[s % 4], c)
        arrive(one_in.at[s], slot("one", s))
        two_out[s] = (both(s, g[0], g[1]) + one_in[s, 0].astype(jnp.float32)).astype(jnp.bfloat16)
        send(two_out.at[s], two_in.at[s], slot("two", s), second)
        keep[s] = both(s, y, h) + one_in[s, 1].astype(jnp.float32)

    def plane_rows(zz):
        return pl.ds(pl.multiple_of(zz * LINES * bit, LINES * bit), LINES * bit)

    def sum_second(s):
        arrive(two_in.at[s], slot("two", s))
        total = keep[s] + two_in[s].astype(jnp.float32)
        keep[s] = total
        z_out[s] = total.astype(jnp.bfloat16)
        for i in range(last, 0, -1):
            send(z_out.at[s, plane_rows(nearest[i])], z_in.at[s, z], slot("z", s), along(nearest[i]))

    per = depth // 2
    width = part_mixed.shape[3]

    def product(s, hh, columns):
        block = dec_all[pl.ds(pl.multiple_of(hh * per, per), per), :, :, columns].reshape(half // LINES, width)
        return jnp.dot(combined[s, hh], block, preferred_element_type=jnp.float32)

    def combine(s):
        arrive(z_in.at[s, pl.ds(0, last)], slot("z", s))
        final = keep[s, plane_rows(z)]
        for i in range(1, depth):
            final += z_in[s, nearest[i]].astype(jnp.float32)
        combined[s, h] = final.astype(jnp.bfloat16)
        send(combined.at[s, h], combined.at[s, h], slot("last", s), x_peer)

    def mix(s):
        for n in range(STEPS):
            columns = slice(n * width, (n + 1) * width)
            mixed[s, :, columns] = product(s, h, columns)
        arrive(combined.at[s, 1 - h], slot("last", s))
        theirs = pl.ds(pl.multiple_of((1 - y) * bit, bit), bit)
        for n in range(STEPS):
            columns = slice(n * width, (n + 1) * width)
            mixed[s, :, columns] = mixed[s, :, columns] + product(s, 1 - h, columns)
            part_mixed[s, n] = mixed[s, theirs, columns].astype(jnp.bfloat16)
            send(part_mixed.at[s, n], mixed_in.at[s, n], slot("mixed", s, n), y_peer)

    stored = []

    def store(s):
        mine = pl.ds(pl.multiple_of(y * bit, bit), bit)
        for n in range(STEPS):
            columns = slice(n * width, (n + 1) * width)
            arrive(mixed_in.at[s, n], slot("mixed", s, n))
            result[s, :, columns] = (mixed[s, mine, columns] + mixed_in[s, n].astype(jnp.float32)).astype(jnp.bfloat16)
        stored.append(fetch(result.at[s], out.at[pl.ds(s * bit, bit)]))

    tok_send(0, 0)
    enc_start(0)
    tok_send(0, 1)
    for i in range(PIECES):
        down_send(i)
    share_start()
    enc_start(1)
    tok_send(1, 0)
    tok_send(1, 1)
    for copy in tok_own:
        copy.wait()
    enc_from_y(0, 0)
    enc_from_z(0)
    enc_from_y(1, 0)
    enc_from_y(0, 1)
    tok_wait(0)
    enc_step(0, 0)
    enc_step(1, 0)
    enc_from_z(1)
    dec_middle()
    enc_from_y(1, 1)
    tok_wait(1)
    enc_step(0, 1)
    enc_step(1, 1)
    enc_share(0)
    enc_share(1)
    enc_done(0)
    lat_from_z(0, 0)
    enc_done(1)
    lat_from_z(1, 0)
    dec_near()
    dec_far()
    lat_from_first(0, 0)
    lat_from_z(0, 1)
    lat_from_first(1, 0)
    lat_from_z(0, 2)
    lat_from_first(0, 1)
    lat_from_z(0, 3)
    share_done()
    gate_own.wait()
    up_own.wait()
    lat_from_second(0, 0)
    lat_from_first(0, 2)
    lat_from_z(1, 1)
    lat_from_second(0, 1)
    lat_from_first(0, 3)
    lat_from_z(1, 2)
    lat_from_second(0, 2)
    lat_from_first(1, 1)
    lat_from_z(1, 3)
    lat_from_second(0, 3)
    for s in range(depth):
        lat_from_core(0, s)
    gate_up(0)
    lat_from_first(1, 2)
    down_wait()
    answer_rows(0)
    lat_from_first(1, 3)
    lat_from_second(1, 0)
    lat_from_second(1, 1)
    gate_up(1)
    sum_cores(0)
    lat_from_second(1, 2)
    lat_from_second(1, 3)
    answer_rows(1)
    for s in range(depth):
        lat_from_core(1, s)
    gate_up(2)
    sum_cores(1)
    answer_rows(2)
    sum_first(0)
    gate_up(3)
    sum_cores(2)
    dec_from_z()
    answer_rows(3)
    sum_first(1)
    sum_cores(3)
    sum_second(0)
    sum_first(2)
    sum_second(1)
    dec_from_core()
    sum_first(3)
    combine(0)
    sum_second(2)
    combine(1)
    mix(0)
    sum_second(3)
    mix(1)
    combine(2)
    combine(3)
    mix(2)
    mix(3)
    for s in range(len(stages)):
        store(s)

    for copy, when in lasting + waiting[-RING:]:
        sent(copy, when)
    for copy in stored:
        copy.wait()


def whole_layer(tokens, enc_weight, routes, gates, gate_weight, up_weight, down_weight, dec_weight):
    groups = lax.axis_size("expert")
    depth = groups // (CORES * LINES)
    rows, width = tokens.shape
    half = enc_weight.shape[1]
    hidden = gate_weight.shape[2]
    bf, f32 = jnp.bfloat16, jnp.float32
    band = LINES * CORES
    chunk = half // CHUNKS
    few = rows // HALVES
    columns = dec_weight.shape[1]
    bit = few // PARTS
    stages = HALVES * PARTS
    block = (depth * LINES * bit, half // LINES)
    small = (LINES * bit, half // LINES)
    anywhere = pl.BlockSpec(memory_space=pl.ANY)
    vmem = pl.BlockSpec(memory_space=pltpu.VMEM)
    dma = pltpu.SemaphoreType.DMA
    scratch = [
        pltpu.VMEM((2, LINES, 2 * rows, width // (LINES * depth)), bf),
        pltpu.VMEM(gate_weight.shape[1:], bf),
        pltpu.VMEM(up_weight.shape[1:], bf),
        pltpu.VMEM((2, hidden, half), bf),
        pltpu.VMEM((CHUNKS, 2, LINES, CORES, enc_weight.shape[0], chunk), bf),
        pltpu.VMEM((depth, CORES, *dec_weight.shape), bf),
        pltpu.VMEM((2, HALVES, groups, few, half), bf),
        pltpu.VMEM((groups, 8, rows), f32),
        pltpu.VMEM((groups, 8, rows), f32),
        pltpu.VMEM((rows, groups * 8), f32),
        pltpu.VMEM((2 * rows, half), f32),
        pltpu.VMEM((HALVES, few, half), bf),
        pltpu.VMEM((HALVES, few, half), bf),
        pltpu.VMEM((2, groups * bit, hidden), bf),
        pltpu.VMEM((stages, CORES, LINES, 2, *block), bf),
        pltpu.VMEM((stages, LINES, 2, *block), bf),
        pltpu.VMEM((stages, 2, *block), bf),
        pltpu.VMEM((stages, 2, *block), bf),
        pltpu.VMEM((stages, *block), bf),
        pltpu.VMEM((stages, *block), bf),
        pltpu.VMEM((stages, *block), f32),
        pltpu.VMEM((stages, *block), bf),
        pltpu.VMEM((stages, depth, *small), bf),
        pltpu.VMEM((stages, 2, *small), bf),
        pltpu.VMEM((stages, LINES * bit, columns), f32),
        pltpu.VMEM((stages, STEPS, bit, columns // STEPS), bf),
        pltpu.VMEM((stages, STEPS, bit, columns // STEPS), bf),
        pltpu.VMEM((stages, bit, columns), bf),
        dma((RING + 7,)), dma((80,)), dma((HALVES, depth)), dma((18,)),
    ]
    return pl.pallas_call(
        layer_kernel,
        out_shape=jax.ShapeDtypeStruct((rows, dec_weight.shape[1]), bf),
        in_specs=[anywhere, anywhere, vmem, vmem, anywhere, anywhere, anywhere, anywhere],
        out_specs=anywhere,
        scratch_shapes=scratch,
        compiler_params=pltpu.CompilerParams(
            collective_id=0, has_side_effects=True, vmem_limit_bytes=60 * 1024 * 1024
        ),
    )(tokens, enc_weight, routes.T, gates.T, gate_weight, up_weight, down_weight, dec_weight)


def on_device(tokens, enc_weight, routes, *rest):
    token_count, choice_count = routes.shape
    plan = whole_layer if 2 * choice_count >= lax.axis_size("expert") else exchange_slots
    return plan(tokens, enc_weight, routes, *rest)


def solution(mesh):
    in_specs = (
        P("expert", None),
        P("expert", "hidden"),
        P("expert", None),
        P("expert", None),
        P("expert", None, "hidden"),
        P("expert", None, "hidden"),
        P("expert", None, "hidden"),
        P("expert", "hidden"),
    )
    out_specs = P("expert", "hidden")
    return jax.shard_map(
        on_device, mesh=mesh, in_specs=in_specs, out_specs=out_specs, check_vma=False
    )
```

```python
import jax
import jax.numpy as jnp
from jax import lax
from jax.experimental import pallas as pl
from jax.experimental.pallas import tpu as pltpu
from jax.sharding import PartitionSpec as P


def exchange_slots(tokens, enc_weight, routes, gates, gate_weight, up_weight, down_weight, dec_weight):
    groups = lax.axis_size("expert")
    token_count, choice_count = routes.shape
    capacity = min(token_count, 2 * token_count * choice_count // groups)
    columns = tokens
    latent = jnp.dot(
        columns,
        lax.all_gather(enc_weight, "expert", axis=0, tiled=True),
        preferred_element_type=jnp.float32,
    ).astype(jnp.bfloat16)
    payload = lax.all_gather(latent, "hidden", axis=1, tiled=True)
    chosen = routes.reshape(-1)
    onehot = (chosen[:, None] == jnp.arange(groups, dtype=jnp.int32)[None, :]).astype(jnp.int32)
    position = jnp.sum((jnp.cumsum(onehot, axis=0) - onehot) * onehot, axis=1)
    target = chosen * capacity + position
    source_row = jnp.arange(token_count * choice_count, dtype=jnp.int32) // choice_count
    payload_width = payload.shape[1]
    outgoing = (
        jnp.zeros((groups * capacity, payload_width), jnp.bfloat16)
        .at[target]
        .set(payload[source_row])
    )
    outgoing = outgoing.reshape(groups, capacity, payload_width)
    gate_matrix = gate_weight[0]
    up_matrix = up_weight[0]
    down_matrix = down_weight[0]
    arrived = lax.all_to_all(outgoing, "expert", split_axis=0, concat_axis=0, tiled=True)
    slot_count = arrived.shape[1]
    inputs = arrived.reshape(groups * slot_count, arrived.shape[2])
    gate_part = jnp.dot(inputs, gate_matrix, preferred_element_type=jnp.float32)
    up_part = jnp.dot(inputs, up_matrix, preferred_element_type=jnp.float32)
    activation = (jax.nn.silu(gate_part) * up_part).astype(jnp.bfloat16)
    answer = jnp.dot(
        lax.all_gather(activation, "hidden", axis=1, tiled=True),
        down_matrix,
        preferred_element_type=jnp.float32,
    ).astype(jnp.bfloat16)
    answer = answer.reshape(groups, slot_count, down_matrix.shape[1])
    returned_rows = lax.all_to_all(answer, "expert", split_axis=0, concat_axis=0, tiled=True)
    returned_rows = returned_rows.reshape(groups * capacity, returned_rows.shape[2])
    picked = returned_rows[target].astype(jnp.float32).reshape(token_count, choice_count, -1)
    combined = jnp.sum(picked * gates[:, :, None], axis=1).astype(jnp.bfloat16)
    combined_all = lax.all_gather(combined, "hidden", axis=1, tiled=True)
    columns = combined_all
    return jnp.dot(
        columns,
        lax.all_gather(dec_weight, "expert", axis=0, tiled=True),
        preferred_element_type=jnp.float32,
    ).astype(jnp.bfloat16)


CORES, LINES = 2, 2
MESH = pl.DeviceIdType.MESH


CHUNKS, HALVES, PARTS, PIECES, STEPS, RING = 2, 2, 2, 1, 2, 48
LATENT_FIRST = ((1, 0), (1, 0), (1, 0), (1, 0))
ANSWER_FIRST = ((0, 1), (0, 1), (0, 1), (0, 1))


def layer_kernel(
    tokens_hbm, enc_hbm, routes, gates, gate_hbm, up_hbm, down_hbm, dec_hbm, out,
    tok, gate, up, down, enc_all, dec_all, latents, table, shares_in, shares, acc, part_out, part_in, activation,
    answers, core_in, one_out, one_in, two_out, two_in, keep, z_out, z_in, combined, mixed, part_mixed, mixed_in, result,
    ssem, rsem, lat_z, local_sem,
):
    groups = lax.axis_size("expert")
    depth = groups // (CORES * LINES)
    e = lax.axis_index("expert")
    h = lax.axis_index("hidden")
    c, y, z = e % CORES, (e // CORES) % LINES, e // (CORES * LINES)

    def at(zz, yy, cc):
        return (zz * LINES + yy) * CORES + cc

    orders = []
    for zz in range(depth):
        others = [o for o in range(depth) if o != zz]
        middle = (depth - 1) / 2
        orders.append([zz] + sorted(others, key=lambda o: (abs(o - zz), abs(o - middle))))
    nearest = []
    for s in range(depth):
        pick = jnp.int32(orders[0][s])
        for zz in range(1, depth):
            pick = jnp.where(z == zz, orders[zz][s], pick)
        nearest.append(pick)

    rows = tok.shape[2] // 2
    wide = tok.shape[3]
    few, half = latents.shape[3:]
    bit = few // PARTS
    chunk = half // CHUNKS
    last = depth - 1
    y_peer = (at(z, 1 - y, c), h)
    core_peer = (at(z, y, 1 - c), h)
    x_peer = (e, 1 - h)

    def route(pair, cc):
        along_y = jnp.where(cc == 0, pair[0], pair[1]) == 1
        first = (jnp.where(along_y, at(z, 1 - y, c), e), jnp.where(along_y, h, 1 - h))
        second = (jnp.where(along_y, e, at(z, 1 - y, c)), jnp.where(along_y, 1 - h, h))
        f = (jnp.where(along_y, 1 - y, y), jnp.where(along_y, h, 1 - h))
        g = (jnp.where(along_y, y, 1 - y), jnp.where(along_y, 1 - h, h))
        return first, second, f, g

    waiting, lasting, slots, local = [], [], {}, []

    def slot(*key):
        return rsem.at[slots.setdefault(key, len(slots))]

    def sent(copy, when):
        if when is None:
            copy.wait_send()
        else:
            pl.when(when)(copy.wait_send)

    def send(src, dst, sem, peer, when=None, long=False):
        turn = len(waiting)
        if not long and turn >= RING:
            sent(*waiting[turn - RING])
        copy = pltpu.make_async_remote_copy(
            src_ref=src, dst_ref=dst, send_sem=ssem.at[RING + len(lasting) if long else turn % RING], recv_sem=sem,
            device_id=peer, device_id_type=MESH,
        )
        if when is None:
            copy.start()
        else:
            pl.when(when)(copy.start)
        (lasting if long else waiting).append((copy, when))

    def along(zz):
        return (at(jnp.clip(zz, 0, depth - 1), y, c), h)

    def spread(block, sem, far, long=False):
        for d in far:
            send(block, block, sem, along(z + d), z + d < depth, long)
            send(block, block, sem, along(z - d), z - d >= 0, long)

    def arrive(dst, sem):
        pltpu.make_async_copy(dst, dst, sem).wait()

    def fetch(src, dst):
        copy = pltpu.make_async_copy(src, dst, local_sem.at[len(local)])
        copy.start()
        local.append(copy)
        return copy

    barrier = pltpu.get_barrier_semaphore()
    peers = [((e + d) % groups, h) for d in range(1, groups)] + [x_peer]
    for peer in peers:
        pl.semaphore_signal(barrier, inc=1, device_id=peer, device_id_type=MESH)

    def segment(zz, yy):
        return pl.ds(pl.multiple_of((zz * LINES + yy) * wide, wide), wide)

    enc_own = [
        fetch(enc_hbm.at[:, pl.ds(k * chunk, chunk)], enc_all.at[k, 0, y, c]) for k in range(CHUNKS)
    ]
    pair, twin = z + 1 - 2 * (z % 2), (z + depth // 2) % depth
    planes, pair_planes = (z, twin), (pair, (pair + depth // 2) % depth)
    tok_own = [
        fetch(tokens_hbm.at[:, segment(planes[j], yy)], tok.at[j, yy, pl.ds(0, rows)])
        for j in range(2) for yy in range(LINES)
    ]
    dec_own = fetch(dec_hbm, dec_all.at[z, c])
    part = down.shape[1]
    gate_own = fetch(gate_hbm.at[0], gate)
    up_own = fetch(up_hbm.at[0], up)
    own_down = fetch(down_hbm.at[0, pl.ds(pl.multiple_of(h * part, part), part)], down.at[h])

    expert = lax.broadcasted_iota(jnp.int32, (groups, rows), 0)
    weight = jnp.zeros((groups, rows), jnp.float32)
    for k in range(routes.shape[0]):
        weight += jnp.where(routes[k : k + 1, :] == expert, gates[k : k + 1, :], 0.0)
    for o in range(groups):
        table[o] = jnp.broadcast_to(weight[o : o + 1, :], table.shape[1:])

    pl.semaphore_wait(barrier, len(peers))

    def enc_block(k, j, yy, cc):
        return enc_all.at[k, j, yy, cc]

    def enc_start(k):
        block = enc_block(k, 0, y, c)
        enc_own[k].wait()
        send(block, enc_block(k, 1, y, c), slot("encz", k), along(twin))
        send(block, block, slot("ency", k, 0), y_peer)
        send(block, block, slot("encc", k, 0), core_peer)

    def enc_from_z(k):
        block = enc_block(k, 1, y, c)
        arrive(block, slot("encz", k))
        send(block, block, slot("ency", k, 1), y_peer)
        send(block, block, slot("encc", k, 1), core_peer)

    def enc_from_y(k, j):
        block = enc_block(k, j, 1 - y, c)
        arrive(block, slot("ency", k, j))
        send(block, block, slot("encc", k, j), core_peer)

    def tok_block(j, yy):
        return tok.at[j, yy, pl.ds(rows, rows)]

    def tok_send(j, i):
        yy = y if i == 0 else 1 - y
        send(tokens_hbm.at[:, segment(pair_planes[j], yy)], tok_block(j, yy), slot("tok", j), along(pair))

    def tok_wait(j):
        arrive(tok.at[j, :, pl.ds(rows, rows)], slot("tok", j))

    def enc_step(k, j):
        arrive(enc_all.at[k, j, :, 1 - c], slot("encc", k, j))
        columns = slice(k * chunk, (k + 1) * chunk)
        for i in range(LINES):
            p = jnp.dot(tok[j, i], enc_all[k, j, i].reshape(wide, chunk), preferred_element_type=jnp.float32)
            if i + j == 0:
                acc[:, columns] = p
            else:
                acc[:, columns] = acc[:, columns] + p

    def enc_share(k):
        part_out[k] = acc[rows + k * few : rows + (k + 1) * few, :].astype(jnp.bfloat16)
        send(part_out.at[k], part_in.at[k], slot("part", k), along(pair))

    def lat_block(k, zz, yy, cc, hh):
        return latents.at[hh, k, (zz * CORES + cc) * LINES + yy]

    def enc_done(k):
        arrive(part_in.at[k], slot("part", k))
        mine = acc[k * few : (k + 1) * few, :] + part_in[k].astype(jnp.float32)
        latents[h, k, (z * CORES + c) * LINES + y] = mine.astype(jnp.bfloat16)

    def lat_spread(k):
        block = lat_block(k, z, y, c, h)
        spread(block, lat_z.at[k, z], range(1, depth))

    def lat_from_z(k, s):
        zz = nearest[s]
        block = lat_block(k, zz, y, c, h)
        if s > 0:
            arrive(block, lat_z.at[k, zz])
        first, second, _, _ = route(LATENT_FIRST[s % 4], c)
        send(block, block, slot("lat1", k, s), first)
        send(block, block, slot("lat2", k, s), second)
        send(block, block, slot("lat3", k, s), core_peer)

    def lat_from_first(k, s):
        _, second, f, _ = route(LATENT_FIRST[s % 4], c)
        block = lat_block(k, nearest[s], f[0], c, f[1])
        arrive(block, slot("lat1", k, s))
        send(block, block, slot("lat4", k, s), second)
        send(block, block, slot("lat3", k, s), core_peer)

    def lat_from_second(k, s):
        _, _, _, g = route(LATENT_FIRST[s % 4], c)
        block = lat_block(k, nearest[s], g[0], c, g[1])
        arrive(block, slot("lat2", k, s))
        send(block, block, slot("lat3", k, s), core_peer)
        block = lat_block(k, nearest[s], 1 - y, c, 1 - h)
        arrive(block, slot("lat4", k, s))
        send(block, block, slot("lat3", k, s), core_peer)

    def lat_from_core(k, s):
        start = (nearest[s] * CORES + 1 - c) * LINES
        arrive(latents.at[:, k, pl.ds(start, LINES)], slot("lat3", k, s))

    def dec_block(zz, cc):
        return dec_all.at[zz, cc]

    def dec_middle():
        block, beyond = dec_block(z, c), z - 1 + 2 * (z % 2)
        dec_own.wait()
        send(block, block, slot("decz"), along(beyond), jnp.logical_and(beyond >= 0, beyond < depth), True)

    def dec_near():
        block = dec_block(z, c)
        send(block, block, slot("decz"), along(pair), None, True)
        send(block, block, slot("dec"), core_peer)

    def dec_far():
        spread(dec_block(z, c), slot("decz"), range(2, depth), True)

    def dec_from_z():
        arrive(dec_all.at[pl.ds(0, last), c], slot("decz"))
        for s in range(1, depth):
            block = dec_block(nearest[s], c)
            send(block, block, slot("dec"), core_peer)

    def dec_from_core():
        arrive(dec_all.at[:, 1 - c], slot("dec"))

    piece = part // PIECES

    def down_rows(hh, i, base):
        return pl.ds(pl.multiple_of(base * part + i * piece, piece), piece)

    def down_send(i):
        send(
            down_hbm.at[0, down_rows(h, i, 1 - h)], down.at[h, pl.ds(i * piece, piece)],
            slot("down", i), x_peer, None, True,
        )

    def down_wait():
        own_down.wait()
        for i in range(PIECES):
            arrive(down.at[1 - h, pl.ds(i * piece, piece)], slot("down", i))

    def share_start():
        for d in range(1, groups):
            o = (e + d) % groups
            send(table.at[o], shares_in.at[e], slot("share"), (o, h))
        shares_in[e] = table[e]

    def share_done():
        arrive(shares_in.at[pl.ds(0, groups - 1)], slot("share"))
        shares[...] = jnp.concatenate([shares_in[o] for o in range(groups)], axis=0).T

    group = CORES * dec_all.shape[2]
    tile = LINES * group

    stages = [(k, p) for k in range(HALVES) for p in range(PARTS)]

    def gate_up(s):
        k, p = stages[s]

        @pl.loop(0, gate.shape[1] // tile, unroll=True)
        def _(n):
            columns = pl.ds(pl.multiple_of(n * tile, tile), tile)
            parts = [
                latents[hh, k, :, p * bit : (p + 1) * bit, :].reshape(groups * bit, half) for hh in range(2)
            ]
            inputs = jnp.concatenate(parts, axis=1)
            g = jnp.dot(inputs, gate[:, columns], preferred_element_type=jnp.float32)
            u = jnp.dot(inputs, up[:, columns], preferred_element_type=jnp.float32)
            activation[s % 2, :, columns] = (g / (1.0 + jnp.exp(-g)) * u).astype(jnp.bfloat16)

    def answer_rows(s):
        k, p = stages[s]
        for hh in (1 - h, h):
            @pl.loop(0, half // tile, unroll=True)
            def _(n):
                columns = pl.ds(pl.multiple_of(n * tile, tile), tile)
                a = jnp.dot(activation[s % 2], down[hh, :, columns], preferred_element_type=jnp.float32)
                for b in range(groups):
                    zz, cc, ty = b // (CORES * LINES), b // LINES % CORES, b % LINES
                    j = at(zz, ty, cc) * 8
                    share = shares[k * few + p * bit : k * few + (p + 1) * bit, j : j + 1]
                    block = a[b * bit : (b + 1) * bit] * share
                    for yy in range(LINES):
                        answers[
                            s, cc, yy, hh, pl.ds((zz * LINES + ty) * bit, bit),
                            pl.ds(pl.multiple_of(n * group, group), group),
                        ] = block[:, yy * group : (yy + 1) * group].astype(jnp.bfloat16)

            for yy in range(LINES):
                send(answers.at[s, 1 - c, yy, hh], core_in.at[s, yy, hh], slot("core", s), core_peer)

    def both(s, yy, hh):
        return answers[s, c, yy, hh].astype(jnp.float32) + core_in[s, yy, hh].astype(jnp.float32)

    def sum_cores(s):
        first, _, f, _ = route(ANSWER_FIRST[s % 4], c)
        arrive(core_in.at[s], slot("core", s))
        for i, (yy, hh) in enumerate(((1 - y, 1 - h), f)):
            one_out[s, i] = both(s, yy, hh).astype(jnp.bfloat16)
            send(one_out.at[s, i], one_in.at[s, i], slot("one", s), first)

    def sum_first(s):
        _, second, _, g = route(ANSWER_FIRST[s % 4], c)
        arrive(one_in.at[s], slot("one", s))
        two_out[s] = (both(s, g[0], g[1]) + one_in[s, 0].astype(jnp.float32)).astype(jnp.bfloat16)
        send(two_out.at[s], two_in.at[s], slot("two", s), second)
        keep[s] = both(s, y, h) + one_in[s, 1].astype(jnp.float32)

    def plane_rows(zz):
        return pl.ds(pl.multiple_of(zz * LINES * bit, LINES * bit), LINES * bit)

    def sum_second(s):
        arrive(two_in.at[s], slot("two", s))
        total = keep[s] + two_in[s].astype(jnp.float32)
        keep[s] = total
        z_out[s] = total.astype(jnp.bfloat16)
        for i in range(last, 0, -1):
            send(z_out.at[s, plane_rows(nearest[i])], z_in.at[s, z], slot("z", s), along(nearest[i]))

    per = depth // 2
    width = part_mixed.shape[3]

    def product(s, hh, columns):
        block = dec_all[pl.ds(pl.multiple_of(hh * per, per), per), :, :, columns].reshape(half // LINES, width)
        return jnp.dot(combined[s, hh], block, preferred_element_type=jnp.float32)

    def combine(s):
        arrive(z_in.at[s, pl.ds(0, last)], slot("z", s))
        final = keep[s, plane_rows(z)]
        for i in range(1, depth):
            final += z_in[s, nearest[i]].astype(jnp.float32)
        combined[s, h] = final.astype(jnp.bfloat16)
        send(combined.at[s, h], combined.at[s, h], slot("last", s), x_peer)

    def mix(s):
        for n in range(STEPS):
            columns = slice(n * width, (n + 1) * width)
            mixed[s, :, columns] = product(s, h, columns)
        arrive(combined.at[s, 1 - h], slot("last", s))
        theirs = pl.ds(pl.multiple_of((1 - y) * bit, bit), bit)
        for n in range(STEPS):
            columns = slice(n * width, (n + 1) * width)
            mixed[s, :, columns] = mixed[s, :, columns] + product(s, 1 - h, columns)
            part_mixed[s, n] = mixed[s, theirs, columns].astype(jnp.bfloat16)
            send(part_mixed.at[s, n], mixed_in.at[s, n], slot("mixed", s, n), y_peer)

    stored = []

    def store(s):
        mine = pl.ds(pl.multiple_of(y * bit, bit), bit)
        for n in range(STEPS):
            columns = slice(n * width, (n + 1) * width)
            arrive(mixed_in.at[s, n], slot("mixed", s, n))
            result[s, :, columns] = (mixed[s, mine, columns] + mixed_in[s, n].astype(jnp.float32)).astype(jnp.bfloat16)
        stored.append(fetch(result.at[s], out.at[pl.ds(s * bit, bit)]))

    tok_send(0, 0)
    enc_start(0)
    tok_send(0, 1)
    for i in range(PIECES):
        down_send(i)
    share_start()
    enc_start(1)
    tok_send(1, 0)
    tok_send(1, 1)
    for copy in tok_own:
        copy.wait()
    enc_from_y(0, 0)
    enc_from_z(0)
    enc_from_y(1, 0)
    enc_from_y(0, 1)
    tok_wait(0)
    enc_step(0, 0)
    enc_step(1, 0)
    enc_from_z(1)
    dec_middle()
    enc_from_y(1, 1)
    tok_wait(1)
    enc_step(0, 1)
    enc_step(1, 1)
    enc_share(0)
    enc_share(1)
    enc_done(0)
    lat_spread(0)
    lat_from_z(0, 0)
    enc_done(1)
    lat_from_z(1, 0)
    lat_from_first(0, 0)
    lat_from_z(0, 1)
    lat_from_first(1, 0)
    lat_from_z(0, 2)
    lat_spread(1)
    lat_from_first(0, 1)
    lat_from_z(0, 3)
    share_done()
    gate_own.wait()
    up_own.wait()
    lat_from_second(0, 0)
    lat_from_first(0, 2)
    lat_from_z(1, 1)
    lat_from_second(0, 1)
    lat_from_first(0, 3)
    lat_from_z(1, 2)
    lat_from_second(0, 2)
    lat_from_first(1, 1)
    lat_from_z(1, 3)
    dec_near()
    dec_far()
    lat_from_second(0, 3)
    for s in range(depth):
        lat_from_core(0, s)
    gate_up(0)
    lat_from_first(1, 2)
    down_wait()
    answer_rows(0)
    lat_from_first(1, 3)
    lat_from_second(1, 0)
    lat_from_second(1, 1)
    gate_up(1)
    sum_cores(0)
    lat_from_second(1, 2)
    lat_from_second(1, 3)
    answer_rows(1)
    for s in range(depth):
        lat_from_core(1, s)
    gate_up(2)
    sum_cores(1)
    answer_rows(2)
    sum_first(0)
    gate_up(3)
    sum_cores(2)
    answer_rows(3)
    sum_first(1)
    sum_cores(3)
    sum_second(0)
    sum_first(2)
    sum_second(1)
    dec_from_z()
    sum_first(3)
    dec_from_core()
    combine(0)
    sum_second(2)
    combine(1)
    sum_second(3)
    mix(0)
    mix(1)
    combine(2)
    mix(2)
    combine(3)
    mix(3)
    for s in range(len(stages)):
        store(s)

    for copy, when in lasting + waiting[-RING:]:
        sent(copy, when)
    for copy in stored:
        copy.wait()


def whole_layer(tokens, enc_weight, routes, gates, gate_weight, up_weight, down_weight, dec_weight):
    groups = lax.axis_size("expert")
    depth = groups // (CORES * LINES)
    rows, width = tokens.shape
    half = enc_weight.shape[1]
    hidden = gate_weight.shape[2]
    bf, f32 = jnp.bfloat16, jnp.float32
    band = LINES * CORES
    chunk = half // CHUNKS
    few = rows // HALVES
    columns = dec_weight.shape[1]
    bit = few // PARTS
    stages = HALVES * PARTS
    block = (depth * LINES * bit, half // LINES)
    small = (LINES * bit, half // LINES)
    anywhere = pl.BlockSpec(memory_space=pl.ANY)
    vmem = pl.BlockSpec(memory_space=pltpu.VMEM)
    dma = pltpu.SemaphoreType.DMA
    scratch = [
        pltpu.VMEM((2, LINES, 2 * rows, width // (LINES * depth)), bf),
        pltpu.VMEM(gate_weight.shape[1:], bf),
        pltpu.VMEM(up_weight.shape[1:], bf),
        pltpu.VMEM((2, hidden, half), bf),
        pltpu.VMEM((CHUNKS, 2, LINES, CORES, enc_weight.shape[0], chunk), bf),
        pltpu.VMEM((depth, CORES, *dec_weight.shape), bf),
        pltpu.VMEM((2, HALVES, groups, few, half), bf),
        pltpu.VMEM((groups, 8, rows), f32),
        pltpu.VMEM((groups, 8, rows), f32),
        pltpu.VMEM((rows, groups * 8), f32),
        pltpu.VMEM((2 * rows, half), f32),
        pltpu.VMEM((HALVES, few, half), bf),
        pltpu.VMEM((HALVES, few, half), bf),
        pltpu.VMEM((2, groups * bit, hidden), bf),
        pltpu.VMEM((stages, CORES, LINES, 2, *block), bf),
        pltpu.VMEM((stages, LINES, 2, *block), bf),
        pltpu.VMEM((stages, 2, *block), bf),
        pltpu.VMEM((stages, 2, *block), bf),
        pltpu.VMEM((stages, *block), bf),
        pltpu.VMEM((stages, *block), bf),
        pltpu.VMEM((stages, *block), f32),
        pltpu.VMEM((stages, *block), bf),
        pltpu.VMEM((stages, depth, *small), bf),
        pltpu.VMEM((stages, 2, *small), bf),
        pltpu.VMEM((stages, LINES * bit, columns), f32),
        pltpu.VMEM((stages, STEPS, bit, columns // STEPS), bf),
        pltpu.VMEM((stages, STEPS, bit, columns // STEPS), bf),
        pltpu.VMEM((stages, bit, columns), bf),
        dma((RING + 7,)), dma((80,)), dma((HALVES, depth)), dma((18,)),
    ]
    return pl.pallas_call(
        layer_kernel,
        out_shape=jax.ShapeDtypeStruct((rows, dec_weight.shape[1]), bf),
        in_specs=[anywhere, anywhere, vmem, vmem, anywhere, anywhere, anywhere, anywhere],
        out_specs=anywhere,
        scratch_shapes=scratch,
        compiler_params=pltpu.CompilerParams(
            collective_id=0, has_side_effects=True, vmem_limit_bytes=60 * 1024 * 1024
        ),
    )(tokens, enc_weight, routes.T, gates.T, gate_weight, up_weight, down_weight, dec_weight)


def on_device(tokens, enc_weight, routes, *rest):
    token_count, choice_count = routes.shape
    plan = whole_layer if 2 * choice_count >= lax.axis_size("expert") else exchange_slots
    return plan(tokens, enc_weight, routes, *rest)


def solution(mesh):
    in_specs = (
        P("expert", None),
        P("expert", "hidden"),
        P("expert", None),
        P("expert", None),
        P("expert", None, "hidden"),
        P("expert", None, "hidden"),
        P("expert", None, "hidden"),
        P("expert", "hidden"),
    )
    out_specs = P("expert", "hidden")
    return jax.shard_map(
        on_device, mesh=mesh, in_specs=in_specs, out_specs=out_specs, check_vma=False
    )
```

```python
import jax
import jax.numpy as jnp
from jax import lax
from jax.experimental import pallas as pl
from jax.experimental.pallas import tpu as pltpu
from jax.sharding import PartitionSpec as P


def exchange_slots(tokens, enc_weight, routes, gates, gate_weight, up_weight, down_weight, dec_weight):
    groups = lax.axis_size("expert")
    token_count, choice_count = routes.shape
    capacity = min(token_count, 2 * token_count * choice_count // groups)
    columns = tokens
    latent = jnp.dot(
        columns,
        lax.all_gather(enc_weight, "expert", axis=0, tiled=True),
        preferred_element_type=jnp.float32,
    ).astype(jnp.bfloat16)
    payload = lax.all_gather(latent, "hidden", axis=1, tiled=True)
    chosen = routes.reshape(-1)
    onehot = (chosen[:, None] == jnp.arange(groups, dtype=jnp.int32)[None, :]).astype(jnp.int32)
    position = jnp.sum((jnp.cumsum(onehot, axis=0) - onehot) * onehot, axis=1)
    target = chosen * capacity + position
    source_row = jnp.arange(token_count * choice_count, dtype=jnp.int32) // choice_count
    payload_width = payload.shape[1]
    outgoing = (
        jnp.zeros((groups * capacity, payload_width), jnp.bfloat16)
        .at[target]
        .set(payload[source_row])
    )
    outgoing = outgoing.reshape(groups, capacity, payload_width)
    gate_matrix = gate_weight[0]
    up_matrix = up_weight[0]
    down_matrix = down_weight[0]
    arrived = lax.all_to_all(outgoing, "expert", split_axis=0, concat_axis=0, tiled=True)
    slot_count = arrived.shape[1]
    inputs = arrived.reshape(groups * slot_count, arrived.shape[2])
    gate_part = jnp.dot(inputs, gate_matrix, preferred_element_type=jnp.float32)
    up_part = jnp.dot(inputs, up_matrix, preferred_element_type=jnp.float32)
    activation = (jax.nn.silu(gate_part) * up_part).astype(jnp.bfloat16)
    answer = jnp.dot(
        lax.all_gather(activation, "hidden", axis=1, tiled=True),
        down_matrix,
        preferred_element_type=jnp.float32,
    ).astype(jnp.bfloat16)
    answer = answer.reshape(groups, slot_count, down_matrix.shape[1])
    returned_rows = lax.all_to_all(answer, "expert", split_axis=0, concat_axis=0, tiled=True)
    returned_rows = returned_rows.reshape(groups * capacity, returned_rows.shape[2])
    picked = returned_rows[target].astype(jnp.float32).reshape(token_count, choice_count, -1)
    combined = jnp.sum(picked * gates[:, :, None], axis=1).astype(jnp.bfloat16)
    combined_all = lax.all_gather(combined, "hidden", axis=1, tiled=True)
    columns = combined_all
    return jnp.dot(
        columns,
        lax.all_gather(dec_weight, "expert", axis=0, tiled=True),
        preferred_element_type=jnp.float32,
    ).astype(jnp.bfloat16)


CORES, LINES = 2, 2
MESH = pl.DeviceIdType.MESH


CHUNKS, HALVES, PARTS, PIECES, STEPS, RING = 2, 2, 2, 1, 2, 40
LATENT_FIRST = ((1, 0), (1, 0), (1, 0), (1, 0))
ANSWER_FIRST = ((0, 1), (0, 1), (0, 1), (0, 1))


def layer_kernel(
    tokens_hbm, enc_hbm, routes, gates, gate_hbm, up_hbm, down_hbm, dec_hbm, out,
    tok, gate, up, down, enc_all, dec_all, latents, table, shares_in, shares, acc, part_out, part_in, activation,
    answers, core_in, one_out, one_in, two_out, two_in, keep, z_out, z_in, combined, mixed, part_mixed, mixed_in, result,
    ssem, rsem, lat_z, local_sem,
):
    groups = lax.axis_size("expert")
    depth = groups // (CORES * LINES)
    e = lax.axis_index("expert")
    h = lax.axis_index("hidden")
    c, y, z = e % CORES, (e // CORES) % LINES, e // (CORES * LINES)

    def at(zz, yy, cc):
        return (zz * LINES + yy) * CORES + cc

    orders = []
    for zz in range(depth):
        others = [o for o in range(depth) if o != zz]
        middle = (depth - 1) / 2
        orders.append([zz] + sorted(others, key=lambda o: (abs(o - zz), abs(o - middle))))
    nearest = []
    for s in range(depth):
        pick = jnp.int32(orders[0][s])
        for zz in range(1, depth):
            pick = jnp.where(z == zz, orders[zz][s], pick)
        nearest.append(pick)

    rows = tok.shape[2] // 2
    wide = tok.shape[3]
    few, half = latents.shape[3:]
    bit = few // PARTS
    chunk = half // CHUNKS
    last = depth - 1
    y_peer = (at(z, 1 - y, c), h)
    core_peer = (at(z, y, 1 - c), h)
    x_peer = (e, 1 - h)

    def route(pair, cc):
        along_y = jnp.where(cc == 0, pair[0], pair[1]) == 1
        first = (jnp.where(along_y, at(z, 1 - y, c), e), jnp.where(along_y, h, 1 - h))
        second = (jnp.where(along_y, e, at(z, 1 - y, c)), jnp.where(along_y, 1 - h, h))
        f = (jnp.where(along_y, 1 - y, y), jnp.where(along_y, h, 1 - h))
        g = (jnp.where(along_y, y, 1 - y), jnp.where(along_y, 1 - h, h))
        return first, second, f, g

    waiting, lasting, slots, local = [], [], {}, []

    def slot(*key):
        return rsem.at[slots.setdefault(key, len(slots))]

    def sent(copy, when):
        if when is None:
            copy.wait_send()
        else:
            pl.when(when)(copy.wait_send)

    def send(src, dst, sem, peer, when=None, long=False):
        turn = len(waiting)
        if not long and turn >= RING:
            sent(*waiting[turn - RING])
        copy = pltpu.make_async_remote_copy(
            src_ref=src, dst_ref=dst, send_sem=ssem.at[RING + len(lasting) if long else turn % RING], recv_sem=sem,
            device_id=peer, device_id_type=MESH,
        )
        if when is None:
            copy.start()
        else:
            pl.when(when)(copy.start)
        (lasting if long else waiting).append((copy, when))

    def along(zz):
        return (at(jnp.clip(zz, 0, depth - 1), y, c), h)

    def spread(block, sem, far, long=False):
        for d in far:
            send(block, block, sem, along(z + d), z + d < depth, long)
            send(block, block, sem, along(z - d), z - d >= 0, long)

    def arrive(dst, sem):
        pltpu.make_async_copy(dst, dst, sem).wait()

    def fetch(src, dst):
        copy = pltpu.make_async_copy(src, dst, local_sem.at[len(local)])
        copy.start()
        local.append(copy)
        return copy

    barrier = pltpu.get_barrier_semaphore()
    peers = [((e + d) % groups, h) for d in range(1, groups)] + [x_peer]
    for peer in peers:
        pl.semaphore_signal(barrier, inc=1, device_id=peer, device_id_type=MESH)

    def segment(zz, yy):
        return pl.ds(pl.multiple_of((zz * LINES + yy) * wide, wide), wide)

    enc_own = [
        fetch(enc_hbm.at[:, pl.ds(k * chunk, chunk)], enc_all.at[k, 0, y, c]) for k in range(CHUNKS)
    ]
    pair, twin = z + 1 - 2 * (z % 2), (z + depth // 2) % depth
    planes, pair_planes = (z, twin), (pair, (pair + depth // 2) % depth)
    tok_own = [
        fetch(tokens_hbm.at[:, segment(planes[j], yy)], tok.at[j, yy, pl.ds(0, rows)])
        for j in range(2) for yy in range(LINES)
    ]
    dec_own = fetch(dec_hbm, dec_all.at[z, c])
    part = down.shape[1]
    gate_own = fetch(gate_hbm.at[0], gate)
    up_own = fetch(up_hbm.at[0], up)
    own_down = fetch(down_hbm.at[0, pl.ds(pl.multiple_of(h * part, part), part)], down.at[h])

    expert = lax.broadcasted_iota(jnp.int32, (groups, rows), 0)
    weight = jnp.zeros((groups, rows), jnp.float32)
    for k in range(routes.shape[0]):
        weight += jnp.where(routes[k : k + 1, :] == expert, gates[k : k + 1, :], 0.0)
    for o in range(groups):
        table[o] = jnp.broadcast_to(weight[o : o + 1, :], table.shape[1:])

    pl.semaphore_wait(barrier, len(peers))

    def enc_block(k, j, yy, cc):
        return enc_all.at[k, j, yy, cc]

    def enc_start(k):
        block = enc_block(k, 0, y, c)
        enc_own[k].wait()
        send(block, enc_block(k, 1, y, c), slot("encz", k), along(twin))
        send(block, block, slot("ency", k, 0), y_peer)
        send(block, block, slot("encc", k, 0), core_peer)

    def enc_from_z(k):
        block = enc_block(k, 1, y, c)
        arrive(block, slot("encz", k))
        send(block, block, slot("ency", k, 1), y_peer)
        send(block, block, slot("encc", k, 1), core_peer)

    def enc_from_y(k, j):
        block = enc_block(k, j, 1 - y, c)
        arrive(block, slot("ency", k, j))
        send(block, block, slot("encc", k, j), core_peer)

    def tok_block(j, yy):
        return tok.at[j, yy, pl.ds(rows, rows)]

    def tok_send(j, i):
        yy = y if i == 0 else 1 - y
        send(tokens_hbm.at[:, segment(pair_planes[j], yy)], tok_block(j, yy), slot("tok", j), along(pair))

    def tok_wait(j):
        arrive(tok.at[j, :, pl.ds(rows, rows)], slot("tok", j))

    def enc_step(k, j):
        arrive(enc_all.at[k, j, :, 1 - c], slot("encc", k, j))
        columns = slice(k * chunk, (k + 1) * chunk)
        for i in range(LINES):
            p = jnp.dot(tok[j, i], enc_all[k, j, i].reshape(wide, chunk), preferred_element_type=jnp.float32)
            if i + j == 0:
                acc[:, columns] = p
            else:
                acc[:, columns] = acc[:, columns] + p

    def enc_share(k):
        part_out[k] = acc[rows + k * few : rows + (k + 1) * few, :].astype(jnp.bfloat16)
        send(part_out.at[k], part_in.at[k], slot("part", k), along(pair))

    def lat_block(k, zz, yy, cc, hh):
        return latents.at[hh, k, (zz * CORES + cc) * LINES + yy]

    def enc_done(k):
        arrive(part_in.at[k], slot("part", k))
        mine = acc[k * few : (k + 1) * few, :] + part_in[k].astype(jnp.float32)
        latents[h, k, (z * CORES + c) * LINES + y] = mine.astype(jnp.bfloat16)

    def lat_spread(k):
        block = lat_block(k, z, y, c, h)
        spread(block, lat_z.at[k, z], range(1, depth))

    def lat_from_z(k, s):
        zz = nearest[s]
        block = lat_block(k, zz, y, c, h)
        if s > 0:
            arrive(block, lat_z.at[k, zz])
        first, second, _, _ = route(LATENT_FIRST[s % 4], c)
        send(block, block, slot("lat1", k, s), first)
        send(block, block, slot("lat2", k, s), second)
        send(block, block, slot("lat3", k, s), core_peer)

    def lat_from_first(k, s):
        _, second, f, _ = route(LATENT_FIRST[s % 4], c)
        block = lat_block(k, nearest[s], f[0], c, f[1])
        arrive(block, slot("lat1", k, s))
        send(block, block, slot("lat4", k, s), second)
        send(block, block, slot("lat3", k, s), core_peer)

    def lat_from_second(k, s):
        _, _, _, g = route(LATENT_FIRST[s % 4], c)
        block = lat_block(k, nearest[s], g[0], c, g[1])
        arrive(block, slot("lat2", k, s))
        send(block, block, slot("lat3", k, s), core_peer)
        block = lat_block(k, nearest[s], 1 - y, c, 1 - h)
        arrive(block, slot("lat4", k, s))
        send(block, block, slot("lat3", k, s), core_peer)

    def lat_from_core(k, s):
        start = (nearest[s] * CORES + 1 - c) * LINES
        arrive(latents.at[:, k, pl.ds(start, LINES)], slot("lat3", k, s))

    def dec_block(zz, cc):
        return dec_all.at[zz, cc]

    def dec_middle():
        block, beyond = dec_block(z, c), z - 1 + 2 * (z % 2)
        dec_own.wait()
        send(block, block, slot("decz"), along(beyond), jnp.logical_and(beyond >= 0, beyond < depth), True)

    def dec_near():
        block = dec_block(z, c)
        send(block, block, slot("decz"), along(pair), None, True)
        send(block, block, slot("dec"), core_peer)

    def dec_far():
        spread(dec_block(z, c), slot("decz"), range(2, depth), True)

    def dec_from_z():
        arrive(dec_all.at[pl.ds(0, last), c], slot("decz"))
        for s in range(1, depth):
            block = dec_block(nearest[s], c)
            send(block, block, slot("dec"), core_peer)

    def dec_from_core():
        arrive(dec_all.at[:, 1 - c], slot("dec"))

    piece = part // PIECES

    def down_rows(hh, i, base):
        return pl.ds(pl.multiple_of(base * part + i * piece, piece), piece)

    def down_send(i):
        send(
            down_hbm.at[0, down_rows(h, i, 1 - h)], down.at[h, pl.ds(i * piece, piece)],
            slot("down", i), x_peer, None, True,
        )

    def down_wait():
        own_down.wait()
        for i in range(PIECES):
            arrive(down.at[1 - h, pl.ds(i * piece, piece)], slot("down", i))

    def share_start():
        for d in range(1, groups):
            o = (e + d) % groups
            send(table.at[o], shares_in.at[e], slot("share"), (o, h))
        shares_in[e] = table[e]

    def share_done():
        arrive(shares_in.at[pl.ds(0, groups - 1)], slot("share"))
        shares[...] = jnp.concatenate([shares_in[o] for o in range(groups)], axis=0).T

    group = CORES * dec_all.shape[2]
    tile = LINES * group

    stages = [(k, p) for k in range(HALVES) for p in range(PARTS)]

    def gate_up(s):
        k, p = stages[s]

        @pl.loop(0, gate.shape[1] // tile, unroll=True)
        def _(n):
            columns = pl.ds(pl.multiple_of(n * tile, tile), tile)
            parts = [
                latents[hh, k, :, p * bit : (p + 1) * bit, :].reshape(groups * bit, half) for hh in range(2)
            ]
            inputs = jnp.concatenate(parts, axis=1)
            g = jnp.dot(inputs, gate[:, columns], preferred_element_type=jnp.float32)
            u = jnp.dot(inputs, up[:, columns], preferred_element_type=jnp.float32)
            activation[s % 2, :, columns] = (g / (1.0 + jnp.exp(-g)) * u).astype(jnp.bfloat16)

    def answer_rows(s):
        k, p = stages[s]
        for hh in (1 - h, h):
            @pl.loop(0, half // tile, unroll=True)
            def _(n):
                columns = pl.ds(pl.multiple_of(n * tile, tile), tile)
                a = jnp.dot(activation[s % 2], down[hh, :, columns], preferred_element_type=jnp.float32)
                for b in range(groups):
                    zz, cc, ty = b // (CORES * LINES), b // LINES % CORES, b % LINES
                    j = at(zz, ty, cc) * 8
                    share = shares[k * few + p * bit : k * few + (p + 1) * bit, j : j + 1]
                    block = a[b * bit : (b + 1) * bit] * share
                    for yy in range(LINES):
                        answers[
                            s, cc, yy, hh, pl.ds((zz * LINES + ty) * bit, bit),
                            pl.ds(pl.multiple_of(n * group, group), group),
                        ] = block[:, yy * group : (yy + 1) * group].astype(jnp.bfloat16)

            for yy in range(LINES):
                send(answers.at[s, 1 - c, yy, hh], core_in.at[s, yy, hh], slot("core", s), core_peer)

    def both(s, yy, hh):
        return answers[s, c, yy, hh].astype(jnp.float32) + core_in[s, yy, hh].astype(jnp.float32)

    def sum_cores(s):
        first, _, f, _ = route(ANSWER_FIRST[s % 4], c)
        arrive(core_in.at[s], slot("core", s))
        for i, (yy, hh) in enumerate(((1 - y, 1 - h), f)):
            one_out[s, i] = both(s, yy, hh).astype(jnp.bfloat16)
            send(one_out.at[s, i], one_in.at[s, i], slot("one", s), first)

    def sum_first(s):
        _, second, _, g = route(ANSWER_FIRST[s % 4], c)
        arrive(one_in.at[s], slot("one", s))
        two_out[s] = (both(s, g[0], g[1]) + one_in[s, 0].astype(jnp.float32)).astype(jnp.bfloat16)
        send(two_out.at[s], two_in.at[s], slot("two", s), second)
        keep[s] = both(s, y, h) + one_in[s, 1].astype(jnp.float32)

    def plane_rows(zz):
        return pl.ds(pl.multiple_of(zz * LINES * bit, LINES * bit), LINES * bit)

    def sum_second(s):
        arrive(two_in.at[s], slot("two", s))
        total = keep[s] + two_in[s].astype(jnp.float32)
        keep[s] = total
        z_out[s] = total.astype(jnp.bfloat16)
        for i in range(last, 0, -1):
            send(z_out.at[s, plane_rows(nearest[i])], z_in.at[s, z], slot("z", s), along(nearest[i]))

    per = depth // 2
    width = part_mixed.shape[3]

    def product(s, hh, columns):
        block = dec_all[pl.ds(pl.multiple_of(hh * per, per), per), :, :, columns].reshape(half // LINES, width)
        return jnp.dot(combined[s, hh], block, preferred_element_type=jnp.float32)

    def combine(s):
        arrive(z_in.at[s, pl.ds(0, last)], slot("z", s))
        final = keep[s, plane_rows(z)]
        for i in range(1, depth):
            final += z_in[s, nearest[i]].astype(jnp.float32)
        combined[s, h] = final.astype(jnp.bfloat16)
        send(combined.at[s, h], combined.at[s, h], slot("last", s), x_peer)

    def mix(s):
        for n in range(STEPS):
            columns = slice(n * width, (n + 1) * width)
            mixed[s, :, columns] = product(s, h, columns)
        arrive(combined.at[s, 1 - h], slot("last", s))
        theirs = pl.ds(pl.multiple_of((1 - y) * bit, bit), bit)
        for n in range(STEPS):
            columns = slice(n * width, (n + 1) * width)
            mixed[s, :, columns] = mixed[s, :, columns] + product(s, 1 - h, columns)
            part_mixed[s, n] = mixed[s, theirs, columns].astype(jnp.bfloat16)
            send(part_mixed.at[s, n], mixed_in.at[s, n], slot("mixed", s, n), y_peer)

    stored = []

    def store(s):
        mine = pl.ds(pl.multiple_of(y * bit, bit), bit)
        for n in range(STEPS):
            columns = slice(n * width, (n + 1) * width)
            arrive(mixed_in.at[s, n], slot("mixed", s, n))
            result[s, :, columns] = (mixed[s, mine, columns] + mixed_in[s, n].astype(jnp.float32)).astype(jnp.bfloat16)
        stored.append(fetch(result.at[s], out.at[pl.ds(s * bit, bit)]))

    tok_send(0, 0)
    enc_start(0)
    tok_send(0, 1)
    for i in range(PIECES):
        down_send(i)
    enc_start(1)
    tok_send(1, 0)
    tok_send(1, 1)
    for copy in tok_own:
        copy.wait()
    enc_from_y(0, 0)
    share_start()
    enc_from_z(0)
    enc_from_y(1, 0)
    enc_from_y(0, 1)
    tok_wait(0)
    enc_step(0, 0)
    enc_step(1, 0)
    enc_from_z(1)
    dec_middle()
    enc_from_y(1, 1)
    tok_wait(1)
    enc_step(0, 1)
    enc_step(1, 1)
    enc_share(0)
    enc_share(1)
    enc_done(0)
    lat_spread(0)
    lat_from_z(0, 0)
    enc_done(1)
    lat_from_z(1, 0)
    lat_from_first(0, 0)
    lat_from_z(0, 1)
    lat_from_first(1, 0)
    lat_from_z(0, 2)
    lat_spread(1)
    lat_from_first(0, 1)
    lat_from_z(0, 3)
    share_done()
    gate_own.wait()
    up_own.wait()
    lat_from_second(0, 0)
    lat_from_first(0, 2)
    lat_from_z(1, 1)
    lat_from_second(0, 1)
    lat_from_first(0, 3)
    lat_from_z(1, 2)
    lat_from_second(0, 2)
    lat_from_first(1, 1)
    lat_from_z(1, 3)
    dec_near()
    dec_far()
    lat_from_second(0, 3)
    for s in range(depth):
        lat_from_core(0, s)
    gate_up(0)
    lat_from_first(1, 2)
    down_wait()
    answer_rows(0)
    lat_from_first(1, 3)
    lat_from_second(1, 0)
    lat_from_second(1, 1)
    gate_up(1)
    sum_cores(0)
    lat_from_second(1, 2)
    lat_from_second(1, 3)
    answer_rows(1)
    for s in range(depth):
        lat_from_core(1, s)
    gate_up(2)
    sum_cores(1)
    answer_rows(2)
    sum_first(0)
    gate_up(3)
    sum_cores(2)
    answer_rows(3)
    sum_cores(3)
    sum_first(1)
    sum_second(0)
    sum_first(2)
    sum_second(1)
    dec_from_z()
    sum_first(3)
    dec_from_core()
    combine(0)
    sum_second(2)
    combine(1)
    sum_second(3)
    mix(0)
    mix(1)
    combine(2)
    mix(2)
    combine(3)
    mix(3)
    for s in range(len(stages)):
        store(s)

    for copy, when in lasting + waiting[-RING:]:
        sent(copy, when)
    for copy in stored:
        copy.wait()


def whole_layer(tokens, enc_weight, routes, gates, gate_weight, up_weight, down_weight, dec_weight):
    groups = lax.axis_size("expert")
    depth = groups // (CORES * LINES)
    rows, width = tokens.shape
    half = enc_weight.shape[1]
    hidden = gate_weight.shape[2]
    bf, f32 = jnp.bfloat16, jnp.float32
    band = LINES * CORES
    chunk = half // CHUNKS
    few = rows // HALVES
    columns = dec_weight.shape[1]
    bit = few // PARTS
    stages = HALVES * PARTS
    block = (depth * LINES * bit, half // LINES)
    small = (LINES * bit, half // LINES)
    anywhere = pl.BlockSpec(memory_space=pl.ANY)
    vmem = pl.BlockSpec(memory_space=pltpu.VMEM)
    dma = pltpu.SemaphoreType.DMA
    scratch = [
        pltpu.VMEM((2, LINES, 2 * rows, width // (LINES * depth)), bf),
        pltpu.VMEM(gate_weight.shape[1:], bf),
        pltpu.VMEM(up_weight.shape[1:], bf),
        pltpu.VMEM((2, hidden, half), bf),
        pltpu.VMEM((CHUNKS, 2, LINES, CORES, enc_weight.shape[0], chunk), bf),
        pltpu.VMEM((depth, CORES, *dec_weight.shape), bf),
        pltpu.VMEM((2, HALVES, groups, few, half), bf),
        pltpu.VMEM((groups, 8, rows), f32),
        pltpu.VMEM((groups, 8, rows), f32),
        pltpu.VMEM((rows, groups * 8), f32),
        pltpu.VMEM((2 * rows, half), f32),
        pltpu.VMEM((HALVES, few, half), bf),
        pltpu.VMEM((HALVES, few, half), bf),
        pltpu.VMEM((2, groups * bit, hidden), bf),
        pltpu.VMEM((stages, CORES, LINES, 2, *block), bf),
        pltpu.VMEM((stages, LINES, 2, *block), bf),
        pltpu.VMEM((stages, 2, *block), bf),
        pltpu.VMEM((stages, 2, *block), bf),
        pltpu.VMEM((stages, *block), bf),
        pltpu.VMEM((stages, *block), bf),
        pltpu.VMEM((stages, *block), f32),
        pltpu.VMEM((stages, *block), bf),
        pltpu.VMEM((stages, depth, *small), bf),
        pltpu.VMEM((stages, 2, *small), bf),
        pltpu.VMEM((stages, LINES * bit, columns), f32),
        pltpu.VMEM((stages, STEPS, bit, columns // STEPS), bf),
        pltpu.VMEM((stages, STEPS, bit, columns // STEPS), bf),
        pltpu.VMEM((stages, bit, columns), bf),
        dma((RING + 7,)), dma((78,)), dma((HALVES, depth)), dma((14,)),
    ]
    return pl.pallas_call(
        layer_kernel,
        out_shape=jax.ShapeDtypeStruct((rows, dec_weight.shape[1]), bf),
        in_specs=[anywhere, anywhere, vmem, vmem, anywhere, anywhere, anywhere, anywhere],
        out_specs=anywhere,
        scratch_shapes=scratch,
        compiler_params=pltpu.CompilerParams(
            collective_id=0, has_side_effects=True, vmem_limit_bytes=60 * 1024 * 1024
        ),
    )(tokens, enc_weight, routes.T, gates.T, gate_weight, up_weight, down_weight, dec_weight)


def on_device(tokens, enc_weight, routes, *rest):
    token_count, choice_count = routes.shape
    plan = whole_layer if 2 * choice_count >= lax.axis_size("expert") else exchange_slots
    return plan(tokens, enc_weight, routes, *rest)


def solution(mesh):
    in_specs = (
        P("expert", None),
        P("expert", "hidden"),
        P("expert", None),
        P("expert", None),
        P("expert", None, "hidden"),
        P("expert", None, "hidden"),
        P("expert", None, "hidden"),
        P("expert", "hidden"),
    )
    out_specs = P("expert", "hidden")
    return jax.shard_map(
        on_device, mesh=mesh, in_specs=in_specs, out_specs=out_specs, check_vma=False
    )
```
